256 devices in a mesh: blk: 64 (over x, z, core), tm: 4 (over y).
Axes of the slice: x: 4, y: 4, z: 8, core: 2. Of those that a mesh axis runs over, the one named last changes fastest.
Arguments:
- density: bfloat16 [6144, 256, 128], P('blk', 'tm'), may hold values from 0.5 to 2
- flow_rest: bfloat16 [6144, 4, 256, 128], P('blk', None, 'tm'), may hold values from -6 to 6
- dest: int32 [6144, 1], P('blk'), may hold values from 0 to 63; in each aligned block of 96 rows (0 to 95, 96 to 191, ...) at most 4 rows name the same one
- weights: bfloat16 [64, 64, 256, 128], P('blk', None, 'tm'), may hold values from -0.001953125 to 0.001953125
- directions: float32 [64, 3], replicated, may hold values from -4 to 4
- bins: int32 [64, 64], P(None, 'blk'), may hold values from 0 to 255
Outputs:
- record: float32 [64, 256], P('blk', 'tm')
The draws below stay inside these ranges and needn't reach their ends.
Inputs may be any that keep to these rules, and one draw needn't show every extreme that they name: `dest`: each row names one source block; the rows of one partition name any block at most 4 times, and some partition names some block exactly 4 times.
All inputs are finite; a program needn't handle non-finite values.
Results may differ from the reference program's by a relative error of at most 0.0003.
Values may be sent and summed in bfloat16 or wider, within the bound.
A program may use at most 128 MiB of HBM per device.

```python
import math
import jax
import jax.numpy as jnp
import numpy as np
from jax import lax

W = 128
NT = 256
NOBS = 64
R_DEV = 96
CAP = 4
ROWS = 6144
N_BLK = 64


def place_ends(result, own_key, low, largest):
    longest = result.shape.index(max(result.shape))
    spots = []
    for shift in (0, 1):
        where = [jax.random.randint(jax.random.fold_in(own_key, axis), (), 0, length) for axis, length in enumerate(result.shape)]
        where[longest] = (where[longest] + shift) % result.shape[longest]
        spots.append(tuple(where))
    return result.at[spots[0]].set(low).at[spots[1]].set(largest)


def raised(drawn, stream_key, source, target, parts, factor):
    owner, partner = [(jnp.arange(drawn.shape[axis_at]) // (drawn.shape[axis_at] // parts)).reshape([-1 if axis == axis_at else 1 for axis in range(drawn.ndim)]) for axis_at in (source, target)]
    chosen = jax.random.permutation(stream_key, parts)[partner]
    strong = (owner == chosen) | (owner == (partner + parts // 2) % parts)
    return jnp.where(strong, factor * drawn, drawn)


def block_levels(rng, shape, split, low, high):
    def one(position, blocks):
        steps = jax.random.uniform(jax.random.fold_in(jax.random.fold_in(rng, 6), position), (blocks,), jnp.float32, low / len(split), high / len(split))
        return jnp.repeat(jnp.exp(steps), shape[position] // blocks).reshape((-1,) + (1,) * (len(shape) - position - 1))

    level = one(*split[0])
    for cut in split[1:]:
        level = level * one(*cut)
    return level


def routed_block(rng, own, number, rows, amount, top, reach, lean):
    sequence = jax.random.permutation(rng, amount)
    packed, usual = load_shares(amount, rows * top, reach, lean, True), load_shares(amount, rows * top, reach, lean, False)
    places = jnp.arange(amount)

    def named(tallies, turn):
        used = int((tallies > 0).sum())
        fixed = max(1, used // 4)
        passed = fixed + (places - fixed + turn * (used - fixed)) % max(1, amount - fixed)
        return jnp.zeros((amount,), jnp.int32).at[sequence[jnp.where(places < fixed, places, passed)]].set(jnp.asarray(tallies, jnp.int32))

    tallies = jnp.where(number % 4 == 0, named(packed, number // 4), named(usual, number - number // 4 - 1))
    mixed = jax.random.permutation(jax.random.fold_in(own, 3), amount)
    source_of, receiver = mixed[0:amount // 2 * 2:2], mixed[1:amount // 2 * 2:2]
    room = jnp.minimum(tallies[source_of] - 1, reach - tallies[receiver]) // 2
    room = jnp.where((source_of == sequence[0]) | (receiver == sequence[0]) | (tallies[receiver] == 0), 0, jnp.maximum(room, 0))
    passed = jax.random.randint(jax.random.fold_in(own, 4), (amount // 2,), 0, 1 << 20) % (room + 1)
    tallies = tallies.at[source_of].add(-passed).at[receiver].add(passed)
    items = jnp.searchsorted(jnp.cumsum(tallies), jnp.arange(rows * top), side="right").astype(jnp.int32)
    listing = items.reshape(top, rows).T
    listing = listing[jax.random.permutation(jax.random.fold_in(own, 1), rows)]
    turn = jax.random.randint(jax.random.fold_in(own, 2), (rows, 1), 0, top)
    return jnp.take_along_axis(listing, (jnp.arange(top)[None, :] + turn) % top, axis=1)


def load_shares(amount, total, reach, lean, full):
    loads = [(1 << 20) // math.isqrt(standing ** lean) + 1 for standing in range(1, amount + 1)]
    largest = reach if full else min(reach, max(-(-total // amount), total * loads[0] // sum(loads)))
    least = 1 if total - largest >= amount - 1 else 0
    counts, spare = [largest] + [least] * (amount - 1), total - largest - least * (amount - 1)
    while spare > 0:
        candidates = [i for i in range(1, amount) if counts[i] < largest] or [i for i in range(1, amount) if counts[i] < reach]
        whole, remaining = sum([loads[i] for i in candidates]), spare
        for i in candidates:
            addition = min(reach - counts[i], max(1, remaining * loads[i] // whole), spare)
            counts[i] = counts[i] + addition
            spare = spare - addition
    return np.array(counts)


def normal_values(stream_key, dims, deviation, reach, split=(), kind=jnp.bfloat16):
    result = jax.random.normal(stream_key, dims, jnp.float32) * deviation
    if len(split) > 0:
        result = block_levels(stream_key, dims, split, -0.22, 0.18) * result
    return jnp.clip(result, min=-reach, max=reach).astype(kind)


def gaussian_with(rng, shape, width, reach, pieces, heavy, held_as=jnp.bfloat16):
    result = width * jax.random.normal(rng, shape, jnp.float32)
    if pieces:
        result = result * block_levels(rng, shape, pieces, -0.22, 0.18)
    return jnp.clip(raised(result, jax.random.fold_in(rng, 3), *heavy), -reach, reach).astype(held_as)


def setup_inputs(seed: int = 0) -> dict:
    streams_of = jax.random.split(jax.random.key(seed), 7)
    density = jnp.clip(jnp.exp(math.log(2.0) - 1.3862944 * jax.random.uniform(streams_of[0], (ROWS, NT, W), jnp.float32) ** block_levels(streams_of[0], (ROWS, NT, W), ((0, 64), (1, 4)), -0.2, 0.2)), 0.5, 2.0).astype(jnp.bfloat16)
    flow_rest = normal_values(streams_of[1], (ROWS, 4, NT, W), 1.0, 6.0, ((0, 64), (2, 4)))
    dest_keys = jax.random.split(jax.random.fold_in(streams_of[2], 1), ROWS // R_DEV)
    dest_turns = jax.random.permutation(jax.random.fold_in(streams_of[2], 3), ROWS // R_DEV)
    dest = jax.vmap(lambda own, number: routed_block(jax.random.fold_in(streams_of[2], 2), own, number, R_DEV, N_BLK, 1, CAP, 2))(dest_keys, dest_turns).reshape((ROWS, 1))
    weights = gaussian_with(streams_of[3], (N_BLK, NOBS, NT, W), (100 * W * ROWS) ** -0.5, 0.001953125, ((0, 64), (2, 4)), (0, 1, 64, 4.0))
    directions = normal_values(streams_of[4], (NOBS, 3), 1.0, 4.0, (), jnp.float32)
    bins = place_ends(jax.random.randint(streams_of[5], (NOBS, N_BLK), 0, NT), jax.random.fold_in(streams_of[5], 1), 0, NT - 1).astype(jnp.int32)
    return {"density": density, "flow_rest": flow_rest, "dest": dest, "weights": weights, "directions": directions, "bins": bins}


def stress_parts(rho, flow):
    speed_x = flow[:, 0]
    speed_y = flow[:, 1]
    speed_z = flow[:, 2]
    excess = flow[:, 3]
    return jnp.stack([rho * speed_x * speed_x + excess, rho * speed_y * speed_y + excess,
                      rho * speed_z * speed_z + excess, rho * speed_x * speed_y,
                      rho * speed_x * speed_z, rho * speed_y * speed_z], axis=1)


def reference(density, flow_rest, dest, weights, directions, bins):
    heading = directions
    projector = jnp.stack([heading[:, 0] * heading[:, 0], heading[:, 1] * heading[:, 1],
                           heading[:, 2] * heading[:, 2], 2.0 * heading[:, 0] * heading[:, 1],
                           2.0 * heading[:, 0] * heading[:, 2], 2.0 * heading[:, 1] * heading[:, 2]], axis=1)

    def per_part(running, index):
        start = (index * R_DEV).astype(jnp.int32)
        dens_part = lax.dynamic_slice_in_dim(density, start, R_DEV, 0).astype(jnp.float32)
        flow_part = lax.dynamic_slice_in_dim(flow_rest, start, R_DEV, 0).astype(jnp.float32)
        targets = lax.dynamic_slice_in_dim(dest[:, 0], start, R_DEV, 0)
        stresses = stress_parts(dens_part, flow_part)
        return running + jax.ops.segment_sum(stresses, targets, num_segments=N_BLK), None

    totals, unused = lax.scan(per_part, jnp.zeros((N_BLK, 6, NT, W), jnp.float32),
                              jnp.arange(N_BLK, dtype=jnp.int32))

    def per_block(pair):
        block_totals, block_weights = pair
        moment = jnp.einsum('oi,itc->otc', projector, block_totals, precision=lax.Precision.HIGHEST)
        return jnp.sum(block_weights.astype(jnp.float32) * moment, axis=2)

    source = lax.map(per_block, (totals, weights))
    curved = jnp.roll(source, -1, axis=2) - 2.0 * source + jnp.roll(source, 1, axis=2)
    lagged = jnp.mod(jnp.arange(NT, dtype=jnp.int32)[None, None, :] - jnp.transpose(bins)[:, :, None], NT).astype(jnp.int32)
    shifted = jnp.take_along_axis(curved, lagged, axis=2)
    return jnp.sum(shifted, axis=0)
```

```python
import functools

import jax
import jax.numpy as jnp
from jax import lax
from jax.experimental import pallas as pl
from jax.experimental.pallas import tpu as pltpu
from jax.sharding import PartitionSpec as P

NX, NZ, NY = 4, 8, 4
ROWS_DEV = 96
SLOTS = 4
NA = 7
NB = 12 - NA
TILES = [(0, i) for i in range(6)] + [(1, i) for i in (5, 4, 3, 2, 1, 0)]
A0, A1, A2 = 0, NA, 2 * NA
B0, B1, B2 = 2 * NA, 2 * NA + NB, 2 * NA + 2 * NB
MESH = pl.DeviceIdType.MESH


def place(j, tile):
    if tile < NA:
        return j * NA + tile
    return 2 * NA + j * NB + tile - NA


def far_first(i, n):
    step = (i + 1) // 2
    return (n // 2 + step * (1 - 2 * (i % 2))) % n


def prep_kernel(dest_ref, bins_ref, list_ref, lag_ref):
    dest = jnp.broadcast_to(dest_ref[...], (ROWS_DEV, 128))
    lane = lax.broadcasted_iota(jnp.int32, (ROWS_DEV, 128), 1)
    row = lax.broadcasted_iota(jnp.int32, (ROWS_DEV, 128), 0)
    hit = dest == lane
    earlier = (
        lax.broadcasted_iota(jnp.int32, (ROWS_DEV, ROWS_DEV), 0)
        > lax.broadcasted_iota(jnp.int32, (ROWS_DEV, ROWS_DEV), 1)
    ).astype(jnp.bfloat16)
    before = jnp.dot(
        earlier, hit.astype(jnp.bfloat16), preferred_element_type=jnp.float32
    ).astype(jnp.int32)
    for s in range(8):
        chosen = jnp.where(hit & (before == s), row, ROWS_DEV)
        list_ref[pl.ds(s, 1), :] = jnp.min(chosen, axis=0, keepdims=True)
    bins = jnp.broadcast_to(bins_ref[...], (64, 128))
    lane64 = lax.broadcasted_iota(jnp.int32, (64, 128), 1) % 64
    row64 = lax.broadcasted_iota(jnp.int32, (64, 128), 0)
    lags = jnp.sum(jnp.where(lane64 == row64, bins, 0), axis=0, keepdims=True)
    lag_ref[...] = jnp.broadcast_to(lags, (8, 128))


def main_kernel(
    list_ref, dir_ref, lag_ref, dens_hbm, flow_hbm, wts_hbm, out_ref,
    dens, flow, C, S, R0, RA1, RA2, RA3, RA4, RB1, RB2, RB3, RB4, W, lag2, G, M, HS, HR,
    ld_sem, s0, r0, sa1, ra1, sa2, ra2, sa3, ra3, sa4, ra4,
    sb1, rb1, sb2, rb2, sb3, rb3, sb4, rb4, sw, rw, sl, rl, sg, rg, sh, rh,
):
    blk = lax.axis_index("blk")
    yy = lax.axis_index("tm")
    c = blk % 2
    chip = blk // 2
    z = chip % NZ
    x = chip // NZ

    def dev(dx, dz, core):
        return (((x + dx) % NX) * NZ + (z + dz) % NZ) * 2 + core

    near_x = (dev(1, 0, c), dev(NX - 1, 0, c))
    near_z = (dev(0, 1, c), dev(0, NZ - 1, c))
    mate = dev(0, 0, 1 - c)

    def remote(src, dst, ssem, rsem, to, ty=None):
        return pltpu.make_async_remote_copy(
            src_ref=src, dst_ref=dst, send_sem=ssem, recv_sem=rsem,
            device_id=(to, yy if ty is None else ty), device_id_type=MESH,
        )

    loads = [
        pltpu.make_async_copy(dens_hbm, dens.at[pl.ds(0, ROWS_DEV)], ld_sem.at[0]),
        pltpu.make_async_copy(flow_hbm, flow.at[pl.ds(0, ROWS_DEV)], ld_sem.at[1]),
        pltpu.make_async_copy(
            wts_hbm.at[0, :, pl.ds(pl.multiple_of(c * 32, 32), 32), :], W.at[c], ld_sem.at[2]
        ),
    ]
    for copy in loads:
        copy.start()

    barrier = pltpu.get_barrier_semaphore()
    for to in near_x + near_z + (mate,):
        pl.semaphore_signal(barrier, inc=1, device_id=(to, yy), device_id_type=MESH)
    for dy in range(1, NY):
        for core in range(2):
            pl.semaphore_signal(
                barrier, inc=1, device_id=(chip * 2 + core, (yy + dy) % NY), device_id_type=MESH
            )
    pl.semaphore_wait(barrier, 5 + 2 * (NY - 1))

    wts_copy = remote(
        wts_hbm.at[0, :, pl.ds(pl.multiple_of((1 - c) * 32, 32), 32), :], W.at[c], sw, rw, mate
    )
    lag_copy = remote(lag_ref, lag2, sl, rl, mate)

    dens[ROWS_DEV] = jnp.zeros((64, 128), jnp.bfloat16)
    flow[ROWS_DEV] = jnp.zeros((4, 64, 128), jnp.bfloat16)
    loads[0].wait()
    loads[1].wait()

    def core_copy(dx, dz):
        return remote(S.at[dx, dz], R0.at[dx, dz], s0.at[dx, dz], r0.at[dx, dz], mate)

    def unit(dx, dz):
        first = dev(dx, dz, 0)
        for j in range(2):
            rows = [list_ref[s, first + j] for s in range(SLOTS)]
            for part in range(2):
                target = C if part == 0 else S
                for chunk in range(2):
                    off = pl.multiple_of(((c + part) % 2) * 32 + chunk * 16, 16)
                    span = pl.ds(off, 16)
                    acc = None
                    for r in rows:
                        rho = dens[r, span, :].astype(jnp.float32)
                        u = flow[r, 0, span, :].astype(jnp.float32)
                        v = flow[r, 1, span, :].astype(jnp.float32)
                        w = flow[r, 2, span, :].astype(jnp.float32)
                        e = flow[r, 3, span, :].astype(jnp.float32)
                        ru, rv, rw_ = rho * u, rho * v, rho * w
                        terms = [ru * u, rv * v, rw_ * w, ru * v, ru * w, rv * w, e]
                        acc = terms if acc is None else [p + q for p, q in zip(acc, terms)]
                    sums = [acc[0] + acc[6], acc[1] + acc[6], acc[2] + acc[6], acc[3], acc[4], acc[5]]
                    for tile, (ch, comp) in enumerate(TILES):
                        if ch == chunk:
                            target[dx, dz, place(j, tile)] = sums[comp]
        core_copy(dx, dz).start()

    def add(dx, dz, lo, hi, *others):
        span = pl.ds(lo, hi - lo)
        total = C[dx, dz, span]
        for ref in others:
            total = total + ref[...]
        C[dx, dz, span] = total

    half_a = ((A0, A1), (A1, A2))
    half_b = ((B0, B1), (B1, B2))

    def src(dx, dz, lo, hi):
        return C.at[dx, dz, pl.ds(lo, hi - lo)]

    def m_a1(d, dz):
        return remote(src(2, dz, *half_a[d]), RA1.at[d, dz], sa1.at[d, dz], ra1.at[d, dz], near_x[d])

    def m_a2(d, dz):
        return remote(src(1 if d == 0 else 3, dz, A0, A2), RA2.at[d, dz], sa2.at[d, dz], ra2.at[d, dz], near_x[d])

    def m_a3(d):
        return remote(src(0, 4, *half_a[d]), RA3.at[d], sa3.at[d], ra3.at[d], near_z[d])

    def m_a4(d, k):
        dz = 3 - k if d == 0 else 5 + k
        return remote(src(0, dz, A0, A2), RA4.at[d, k], sa4.at[d, k], ra4.at[d, k], near_z[d])

    def m_b1(d, dx):
        return remote(src(dx, 4, *half_b[d]), RB1.at[d, dx], sb1.at[d, dx], rb1.at[d, dx], near_z[d])

    def m_b2(d, k, dx):
        dz = 3 - k if d == 0 else 5 + k
        return remote(src(dx, dz, B0, B2), RB2.at[d, k, dx], sb2.at[d, k, dx], rb2.at[d, k, dx], near_z[d])

    def m_b3(d):
        return remote(src(2, 0, *half_b[d]), RB3.at[d], sb3.at[d], rb3.at[d], near_x[d])

    def m_b4(d):
        return remote(src(1 if d == 0 else 3, 0, B0, B2), RB4.at[d], sb4.at[d], rb4.at[d], near_x[d])

    def finish(gp):
        dz = far_first(gp, NZ)

        def step(k, carry):
            dx = far_first(k, NX)
            core_copy(dx, dz).wait_recv()
            add(dx, dz, 0, 24, R0.at[dx, dz])

            @pl.when(k == 0)
            def _():
                m_a1(0, dz).start()
                m_a1(1, dz).start()

            @pl.when(gp == 0)
            def _():
                m_b1(0, dx).start()
                m_b1(1, dx).start()

            return carry

        lax.fori_loop(0, NX, step, 0)

    def ev_a2(dz):
        for d in range(2):
            m_a1(d, dz).wait_recv()
            add(1 if d == 0 else 3, dz, *half_a[d], RA1.at[d, dz])
            m_a2(d, dz).start()

    def ev_b2(k, dx):
        for d in range(2):
            dz = 3 - k if d == 0 else 5 + k
            if k == 0:
                m_b1(d, dx).wait_recv()
                add(dx, dz, *half_b[d], RB1.at[d, dx])
            else:
                m_b2(d, k - 1, dx).wait_recv()
                add(dx, dz, B0, B2, RB2.at[d, k - 1, dx])
            m_b2(d, k, dx).start()

    def ev_ra2(dz):
        m_a2(0, dz).wait_recv()
        m_a2(1, dz).wait_recv()
        add(0, dz, A0, A2, RA2.at[0, dz], RA2.at[1, dz])
        if dz == 4:
            m_a3(0).start()
            m_a3(1).start()
        elif dz == 0:
            m_a4(0, 2).wait_recv()
            m_a4(1, 2).wait_recv()
            add(0, 0, A0, A2, RA4.at[0, 2], RA4.at[1, 2])
        else:
            d, k = (0, 3 - dz) if dz < 4 else (1, dz - 5)
            if k == 0:
                m_a3(d).wait_recv()
                add(0, dz, *half_a[d], RA3.at[d])
            else:
                m_a4(d, k - 1).wait_recv()
                add(0, dz, A0, A2, RA4.at[d, k - 1])
            m_a4(d, k).start()

    def ev_rb2(dx):
        m_b2(0, 2, dx).wait_recv()
        m_b2(1, 2, dx).wait_recv()
        add(dx, 0, B0, B2, RB2.at[0, 2, dx], RB2.at[1, 2, dx])
        if dx == 2:
            m_b3(0).start()
            m_b3(1).start()
        elif dx == 0:
            m_b4(0).wait_recv()
            m_b4(1).wait_recv()
            add(0, 0, B0, B2, RB4.at[0], RB4.at[1])
        else:
            d = 0 if dx == 1 else 1
            m_b3(d).wait_recv()
            add(dx, 0, *half_b[d], RB3.at[d])
            m_b4(d).start()

    def group(g, carry):
        dz = far_first(g, NZ)

        def step(k, inner):
            unit(far_first(k, NX), dz)
            return inner

        lax.fori_loop(0, NX, step, 0)

        @pl.when(g >= 1)
        def _():
            finish(g - 1)

        @pl.when(g == 3)
        def _():
            def send(k, inner):
                ev_b2(0, far_first(k, NX))
                return inner

            lax.fori_loop(0, NX, send, 0)

        @pl.when(g >= 4)
        def _():
            ev_a2(far_first(g - 4, NZ))

        return carry

    lax.fori_loop(0, NZ, group, 0)
    wts_copy.start()
    lag_copy.start()
    finish(NZ - 1)
    ev_b2(1, 2)
    ev_b2(1, 1)
    ev_b2(1, 3)
    ev_a2(6)
    ev_b2(1, 0)
    ev_a2(1)
    ev_b2(2, 2)
    ev_ra2(4)
    ev_b2(2, 1)
    ev_ra2(3)
    ev_b2(2, 3)
    ev_b2(2, 0)
    ev_ra2(5)
    ev_rb2(2)
    ev_a2(7)
    ev_a2(0)
    ev_ra2(2)
    ev_ra2(6)
    ev_ra2(1)
    ev_rb2(1)
    ev_rb2(3)
    ev_ra2(7)
    ev_ra2(0)
    ev_rb2(0)

    loads[2].wait()
    wts_copy.wait()
    lag_copy.wait()
    lane16 = lax.broadcasted_iota(jnp.int32, (16, 128), 1)
    cols = tuple(jnp.zeros((16, 128), jnp.float32) for _ in range(2))
    for j in range(2):
        def project(o, carry):
            d0, d1, d2 = dir_ref[o, 0], dir_ref[o, 1], dir_ref[o, 2]
            coef = [d0 * d0, d1 * d1, d2 * d2, 2.0 * d0 * d1, 2.0 * d0 * d2, 2.0 * d1 * d2]
            new = []
            for chunk in range(2):
                moment = None
                for tile, (ch, comp) in enumerate(TILES):
                    if ch == chunk:
                        term = coef[comp] * C[0, 0, place(j, tile)]
                        moment = term if moment is None else moment + term
                weight = W[j, o, pl.ds(chunk * 16, 16), :].astype(jnp.float32)
                value = jnp.sum(weight * moment, axis=1, keepdims=True)
                new.append(jnp.where(lane16 == j * 64 + o, value, carry[chunk]))
            return tuple(new)

        cols = lax.fori_loop(0, 64, project, cols, unroll=4)

    mine = yy * 2 + c
    G[mine, pl.ds(0, 16), :] = cols[0]
    G[mine, pl.ds(16, 16), :] = cols[1]
    for dy in range(NY):
        for dc in range(2):
            if dy or dc:
                remote(
                    G.at[mine], G.at[mine], sg, rg, chip * 2 + (c + dc) % 2, (yy + dy) % NY
                ).start()
    gathered = remote(G.at[pl.ds(0, 7)], G.at[pl.ds(0, 7)], sg, rg, mate)
    gathered.wait_send()
    gathered.wait_recv()

    period = G[...].reshape(256, 128)
    curved = pltpu.roll(period, 255, 0) - 2.0 * period + pltpu.roll(period, 1, 0)
    lane = lax.broadcasted_iota(jnp.int32, (8, 128), 1)
    lags = jnp.where(lane // 64 == c, lag_ref[...], lag2[...])
    lags = ((lags + 256 - yy * 64) % 256)[0:1, :]
    shifted = curved
    for bit in range(8):
        chosen = jnp.broadcast_to((lags // (1 << bit)) % 2 == 1, (256, 128))
        shifted = jnp.where(chosen, pltpu.roll(shifted, 1 << bit, 0), shifted)
    slab = shifted[0:64, :]
    slab = slab + pltpu.roll(slab, 64, 1)
    M[...] = jnp.transpose(jnp.concatenate([slab, slab], axis=0))
    for i in range(32):
        HS[i] = M[pl.ds(2 * i + c, 1), :]

    def m_h(r):
        to = dev(r // NZ, r % NZ, c)
        return remote(HS.at[to // 2], HR.at[r - 1], sh, rh, to)

    def send(r, carry):
        m_h(r).start()
        return carry

    lax.fori_loop(1, 32, send, 0)

    wait_all = [core_copy(i, j) for i in range(NX) for j in range(NZ)]
    wait_all += [m_a1(d, j) for d in range(2) for j in range(NZ)]
    wait_all += [m_a2(d, j) for d in range(2) for j in range(NZ)]
    wait_all += [m_a3(d) for d in range(2)]
    wait_all += [m_a4(d, k) for d in range(2) for k in range(3)]
    wait_all += [m_b1(d, i) for d in range(2) for i in range(NX)]
    wait_all += [m_b2(d, k, i) for d in range(2) for k in range(3) for i in range(NX)]
    wait_all += [m_b3(d) for d in range(2)]
    wait_all += [m_b4(d) for d in range(2)]
    for copy in wait_all:
        copy.wait_send()

    own = HS[chip]
    scattered = remote(HS.at[pl.ds(0, 31)], HR.at[pl.ds(0, 31)], sh, rh, mate)
    scattered.wait_send()
    scattered.wait_recv()
    total = own + jnp.sum(HR[...], axis=0)
    out_ref[...] = total[:, 0:64]


def body(density, flow_rest, dest, weights, directions, bins):
    lists, lags = pl.pallas_call(
        prep_kernel,
        out_shape=(
            jax.ShapeDtypeStruct((8, 128), jnp.int32),
            jax.ShapeDtypeStruct((8, 128), jnp.int32),
        ),
        name="prep",
    )(dest, bins)
    f32, bf16 = jnp.float32, jnp.bfloat16
    vm, dma = pltpu.VMEM, pltpu.SemaphoreType.DMA
    tile = (16, 128)
    scratch = [
        vm((ROWS_DEV + 1, 64, 128), bf16),
        vm((ROWS_DEV + 1, 4, 64, 128), bf16),
        vm((NX, NZ, 24) + tile, f32),
        vm((NX, NZ, 24) + tile, f32),
        vm((NX, NZ, 24) + tile, f32),
        vm((2, NZ, NA) + tile, f32),
        vm((2, NZ, 2 * NA) + tile, f32),
        vm((2, NA) + tile, f32),
        vm((2, 3, 2 * NA) + tile, f32),
        vm((2, NX, NB) + tile, f32),
        vm((2, 3, NX, 2 * NB) + tile, f32),
        vm((2, NB) + tile, f32),
        vm((2, 2 * NB) + tile, f32),
        vm((2, 64, 32, 128), bf16),
        vm((8, 128), jnp.int32),
        vm((8, 32, 128), f32),
        vm((128, 128), f32),
        vm((32, 1, 128), f32),
        vm((31, 1, 128), f32),
        dma((3,)),
    ]
    for shape in ((NX, NZ), (2, NZ), (2, NZ), (2,), (2, 3), (2, NX), (2, 3, NX), (2,), (2,)):
        scratch += [dma(shape), dma(shape)]
    scratch += [dma(())] * 8
    return pl.pallas_call(
        main_kernel,
        out_shape=jax.ShapeDtypeStruct((1, 64), f32),
        in_specs=[
            pl.BlockSpec(memory_space=pltpu.SMEM),
            pl.BlockSpec(memory_space=pltpu.SMEM),
            pl.BlockSpec(memory_space=pltpu.VMEM),
            pl.BlockSpec(memory_space=pl.ANY),
            pl.BlockSpec(memory_space=pl.ANY),
            pl.BlockSpec(memory_space=pl.ANY),
        ],
        out_specs=pl.BlockSpec(memory_space=pltpu.VMEM),
        scratch_shapes=scratch,
        compiler_params=pltpu.CompilerParams(
            collective_id=0, has_side_effects=True, vmem_limit_bytes=60 << 20
        ),
        name="rotor",
    )(lists, directions, lags, density, flow_rest, weights)


def solution(mesh):
    placed = (
        P("blk", "tm", None),
        P("blk", None, "tm", None),
        P("blk", None),
        P("blk", None, "tm", None),
        P(),
        P(None, "blk"),
    )
    return jax.shard_map(
        body, mesh=mesh, in_specs=placed, out_specs=P("blk", "tm"), check_vma=False
    )
```

```python
import jax
import jax.numpy as jnp
from jax import lax
from jax.experimental import pallas as pl
from jax.experimental.pallas import tpu as pltpu
from jax.sharding import PartitionSpec as P

NX, NZ, NY = 4, 8, 4
ROWS_DEV = 96
SLOTS = 4
NA = 7
NB = 12 - NA
TILES = [(0, i) for i in range(6)] + [(1, i) for i in (5, 4, 3, 2, 1, 0)]
A0, A1, A2 = 0, NA, 2 * NA
B0, B1, B2 = 2 * NA, 2 * NA + NB, 2 * NA + 2 * NB
MESH = pl.DeviceIdType.MESH


def place(j, tile):
    if tile < NA:
        return j * NA + tile
    return 2 * NA + j * NB + tile - NA


def far_first(i, n):
    step = (i + 1) // 2
    return (n // 2 + step * (1 - 2 * (i % 2))) % n


def main_kernel(
    dir_ref, dest_ref, bins_ref, dens_hbm, flow_hbm, wts_hbm, out_ref,
    dens, flow, list_vm, list_ref, lag_ref, C, S, R0, RA1, RA2, RA3, RA4, RB1, RB2, RB3, RB4, W, lag2, Z, G, M, HS, HR,
    ld_sem, s0, r0, sa1, ra1, sa2, ra2, sa3, ra3, sa4, ra4,
    sb1, rb1, sb2, rb2, sb3, rb3, sb4, rb4, sw, rw, sl, rl, sg, rg, sh, rh, met_y, met_mate,
):
    blk = lax.axis_index("blk")
    yy = lax.axis_index("tm")
    c = blk % 2
    chip = blk // 2
    z = chip % NZ
    x = chip // NZ

    def dev(dx, dz, core):
        return (((x + dx) % NX) * NZ + (z + dz) % NZ) * 2 + core

    near_x = (dev(1, 0, c), dev(NX - 1, 0, c))
    near_z = (dev(0, 1, c), dev(0, NZ - 1, c))
    mate = dev(0, 0, 1 - c)

    def remote(src, dst, ssem, rsem, to, ty=None):
        return pltpu.make_async_remote_copy(
            src_ref=src, dst_ref=dst, send_sem=ssem, recv_sem=rsem,
            device_id=(to, yy if ty is None else ty), device_id_type=MESH,
        )

    loads = [
        pltpu.make_async_copy(dens_hbm, dens.at[pl.ds(0, ROWS_DEV)], ld_sem.at[0]),
        pltpu.make_async_copy(flow_hbm, flow.at[pl.ds(0, ROWS_DEV)], ld_sem.at[1]),
        pltpu.make_async_copy(
            wts_hbm.at[0, :, pl.ds(pl.multiple_of(c * 32, 32), 32), :], W.at[c], ld_sem.at[2]
        ),
    ]
    for copy in loads:
        copy.start()

    barrier = pltpu.get_barrier_semaphore()
    along_y = ((yy + 1) % NY, (yy + NY - 1) % NY)
    for to in near_x + near_z + (mate,):
        pl.semaphore_signal(barrier, inc=1, device_id=(to, yy), device_id_type=MESH)
    for to in along_y:
        pl.semaphore_signal(barrier, inc=1, device_id=(blk, to), device_id_type=MESH)

    target = jnp.broadcast_to(dest_ref[...], (64, ROWS_DEV))
    row = lax.broadcasted_iota(jnp.int32, (64, ROWS_DEV), 1)
    hit = target == lax.broadcasted_iota(jnp.int32, (64, ROWS_DEV), 0)
    earlier = lax.broadcasted_iota(jnp.int32, (ROWS_DEV, ROWS_DEV), 0) < lax.broadcasted_iota(
        jnp.int32, (ROWS_DEV, ROWS_DEV), 1
    )
    before = jnp.dot(
        hit.astype(jnp.float32).astype(jnp.bfloat16),
        earlier.astype(jnp.float32).astype(jnp.bfloat16),
        preferred_element_type=jnp.float32,
    ).astype(jnp.int32)
    lane64 = lax.broadcasted_iota(jnp.int32, (64, 128), 1)
    lists = jnp.full((64, 128), ROWS_DEV, jnp.int32)
    for s in range(SLOTS):
        chosen = jnp.min(
            jnp.where(hit & (before == s), row, ROWS_DEV), axis=1, keepdims=True
        )
        lists = jnp.where(lane64 == s, chosen, lists)
    list_vm[...] = lists
    list_copy = pltpu.make_async_copy(list_vm, list_ref, ld_sem.at[3])
    list_copy.start()

    source = lax.broadcasted_iota(jnp.int32, (64, 128), 0)
    wanted = 2 * (lane64 % 32) + lane64 // 64
    spread = jnp.where(
        source == wanted, 1.0, 0.0
    )
    lag_ref[...] = jnp.dot(
        jnp.broadcast_to(bins_ref[...], (8, 64)).astype(jnp.float32).astype(jnp.bfloat16),
        spread.astype(jnp.bfloat16),
        preferred_element_type=jnp.float32,
    ).astype(jnp.int32)

    dens[ROWS_DEV] = jnp.zeros((64, 128), jnp.bfloat16)
    flow[ROWS_DEV] = jnp.zeros((4, 64, 128), jnp.bfloat16)

    pl.semaphore_wait(barrier, 7)
    for to in along_y:
        pl.semaphore_signal(met_y, inc=1, device_id=(blk, to), device_id_type=MESH)

    wts_copy = remote(
        wts_hbm.at[0, :, pl.ds(pl.multiple_of((1 - c) * 32, 32), 32), :], W.at[c], sw, rw, mate
    )
    lag_copy = remote(lag_ref, lag2, sl, rl, mate)

    list_copy.wait()
    loads[0].wait()
    loads[1].wait()

    def core_copy(dx, dz):
        return remote(S.at[dx, dz], R0.at[dx, dz], s0.at[dx, dz], r0.at[dx, dz], mate)

    def unit(dx, dz):
        first = dev(dx, dz, 0)
        for j in range(2):
            rows = [list_ref[first + j, s] for s in range(SLOTS)]
            for part in range(2):
                target = C if part == 0 else S
                for chunk in range(2):
                    off = pl.multiple_of(((c + part) % 2) * 32 + chunk * 16, 16)
                    span = pl.ds(off, 16)
                    acc = None
                    for r in rows:
                        rho = dens[r, span, :].astype(jnp.float32)
                        u = flow[r, 0, span, :].astype(jnp.float32)
                        v = flow[r, 1, span, :].astype(jnp.float32)
                        w = flow[r, 2, span, :].astype(jnp.float32)
                        e = flow[r, 3, span, :].astype(jnp.float32)
                        ru, rv, rw_ = rho * u, rho * v, rho * w
                        terms = [ru * u, rv * v, rw_ * w, ru * v, ru * w, rv * w, e]
                        acc = terms if acc is None else [p + q for p, q in zip(acc, terms)]
                    sums = [acc[0] + acc[6], acc[1] + acc[6], acc[2] + acc[6], acc[3], acc[4], acc[5]]
                    for tile, (ch, comp) in enumerate(TILES):
                        if ch == chunk:
                            target[dx, dz, place(j, tile)] = sums[comp]
        core_copy(dx, dz).start()

    def add(dx, dz, lo, hi, *others):
        span = pl.ds(lo, hi - lo)
        total = C[dx, dz, span]
        for ref in others:
            total = total + ref[...]
        C[dx, dz, span] = total

    half_a = ((A0, A1), (A1, A2))
    half_b = ((B0, B1), (B1, B2))

    def src(dx, dz, lo, hi):
        return C.at[dx, dz, pl.ds(lo, hi - lo)]

    def m_a1(d, dz):
        return remote(src(2, dz, *half_a[d]), RA1.at[d, dz], sa1.at[d, dz], ra1.at[d, dz], near_x[d])

    def m_a2(d, dz):
        return remote(src(1 if d == 0 else 3, dz, A0, A2), RA2.at[d, dz], sa2.at[d, dz], ra2.at[d, dz], near_x[d])

    def m_a3(d):
        return remote(src(0, 4, *half_a[d]), RA3.at[d], sa3.at[d], ra3.at[d], near_z[d])

    def m_a4(d, k):
        dz = 3 - k if d == 0 else 5 + k
        return remote(src(0, dz, A0, A2), RA4.at[d, k], sa4.at[d, k], ra4.at[d, k], near_z[d])

    def m_b1(d, dx):
        return remote(src(dx, 4, *half_b[d]), RB1.at[d, dx], sb1.at[d, dx], rb1.at[d, dx], near_z[d])

    def m_b2(d, k, dx):
        dz = 3 - k if d == 0 else 5 + k
        return remote(src(dx, dz, B0, B2), RB2.at[d, k, dx], sb2.at[d, k, dx], rb2.at[d, k, dx], near_z[d])

    def m_b3(d):
        return remote(src(2, 0, *half_b[d]), RB3.at[d], sb3.at[d], rb3.at[d], near_x[d])

    def m_b4(d):
        return remote(src(1 if d == 0 else 3, 0, B0, B2), RB4.at[d], sb4.at[d], rb4.at[d], near_x[d])

    def finish(gp):
        dz = far_first(gp, NZ)

        def step(k, carry):
            dx = far_first(k, NX)
            core_copy(dx, dz).wait_recv()
            add(dx, dz, 0, 24, R0.at[dx, dz])

            @pl.when(k == 0)
            def _():
                m_a1(0, dz).start()
                m_a1(1, dz).start()

            @pl.when(gp == 0)
            def _():
                m_b1(0, dx).start()
                m_b1(1, dx).start()

            return carry

        lax.fori_loop(0, NX, step, 0)

    def ev_a2(dz):
        for d in range(2):
            m_a1(d, dz).wait_recv()
            add(1 if d == 0 else 3, dz, *half_a[d], RA1.at[d, dz])
            m_a2(d, dz).start()

    def ev_b2(k, dx):
        for d in range(2):
            dz = 3 - k if d == 0 else 5 + k
            if k == 0:
                m_b1(d, dx).wait_recv()
                add(dx, dz, *half_b[d], RB1.at[d, dx])
            else:
                m_b2(d, k - 1, dx).wait_recv()
                add(dx, dz, B0, B2, RB2.at[d, k - 1, dx])
            m_b2(d, k, dx).start()

    def ev_ra2(dz):
        m_a2(0, dz).wait_recv()
        m_a2(1, dz).wait_recv()
        add(0, dz, A0, A2, RA2.at[0, dz], RA2.at[1, dz])
        if dz == 4:
            m_a3(0).start()
            m_a3(1).start()
        elif dz == 0:
            m_a4(0, 2).wait_recv()
            m_a4(1, 2).wait_recv()
            add(0, 0, A0, A2, RA4.at[0, 2], RA4.at[1, 2])
        else:
            d, k = (0, 3 - dz) if dz < 4 else (1, dz - 5)
            if k == 0:
                m_a3(d).wait_recv()
                add(0, dz, *half_a[d], RA3.at[d])
            else:
                m_a4(d, k - 1).wait_recv()
                add(0, dz, A0, A2, RA4.at[d, k - 1])
            m_a4(d, k).start()

    def ev_rb2(dx):
        m_b2(0, 2, dx).wait_recv()
        m_b2(1, 2, dx).wait_recv()
        add(dx, 0, B0, B2, RB2.at[0, 2, dx], RB2.at[1, 2, dx])
        if dx == 2:
            m_b3(0).start()
            m_b3(1).start()
        elif dx == 0:
            m_b4(0).wait_recv()
            m_b4(1).wait_recv()
            add(0, 0, B0, B2, RB4.at[0], RB4.at[1])
        else:
            d = 0 if dx == 1 else 1
            m_b3(d).wait_recv()
            add(dx, 0, *half_b[d], RB3.at[d])
            m_b4(d).start()

    def group(g, carry):
        dz = far_first(g, NZ)

        def step(k, inner):
            unit(far_first(k, NX), dz)
            return inner

        lax.fori_loop(0, NX, step, 0)

        @pl.when(g >= 1)
        def _():
            finish(g - 1)

        @pl.when(g == 3)
        def _():
            def send(k, inner):
                ev_b2(0, far_first(k, NX))
                return inner

            lax.fori_loop(0, NX, send, 0)

        @pl.when(g >= 4)
        def _():
            ev_a2(far_first(g - 4, NZ))

        return carry

    lax.fori_loop(0, NZ, group, 0)
    wts_copy.start()
    lag_copy.start()
    pl.semaphore_wait(met_y, 2)
    pl.semaphore_signal(met_mate, inc=1, device_id=(mate, yy), device_id_type=MESH)
    finish(NZ - 1)
    ev_b2(1, 2)
    ev_b2(1, 1)
    ev_b2(1, 3)
    ev_a2(6)
    ev_b2(1, 0)
    ev_a2(1)
    ev_b2(2, 2)
    ev_ra2(4)
    ev_b2(2, 1)
    ev_ra2(3)
    ev_b2(2, 3)
    ev_b2(2, 0)
    ev_ra2(5)
    ev_rb2(2)
    ev_a2(7)
    ev_a2(0)
    ev_ra2(2)
    ev_ra2(6)
    ev_ra2(1)
    ev_rb2(1)
    ev_rb2(3)
    ev_ra2(7)
    ev_ra2(0)
    ev_rb2(0)

    loads[2].wait()
    wts_copy.wait()
    lag_copy.wait()
    lane16 = lax.broadcasted_iota(jnp.int32, (16, 128), 1)

    def project(o, carry):
        d0, d1, d2 = dir_ref[0, o], dir_ref[1, o], dir_ref[2, o]
        coef = [d0 * d0, d1 * d1, d2 * d2, 2.0 * d0 * d1, 2.0 * d0 * d2, 2.0 * d1 * d2]
        new = []
        for chunk in range(2):
            out = carry[chunk]
            for j in range(2):
                moment = None
                for tile, (ch, comp) in enumerate(TILES):
                    if ch == chunk:
                        term = coef[comp] * C[0, 0, place(j, tile)]
                        moment = term if moment is None else moment + term
                weight = W[j, o, pl.ds(chunk * 16, 16), :].astype(jnp.float32)
                value = jnp.sum(weight * moment, axis=1, keepdims=True)
                out = jnp.where(lane16 == (o % 2) * 64 + j * 32 + o // 2, value, out)
            new.append(out)
        return tuple(new)

    zero = jnp.zeros((16, 128), jnp.float32)
    cols = lax.fori_loop(0, 64, project, (zero, zero), unroll=2)

    low = lane16 < 64
    Z[0] = jnp.where(low, cols[0], pltpu.roll(cols[1], 64, 1))
    Z[1] = jnp.where(low, pltpu.roll(cols[0], 64, 1), cols[1])
    pl.semaphore_wait(met_mate, 1)
    mine = yy * 2 + c
    for dc in range(2):
        for dy in range(NY):
            core = (c + dc) % 2
            if dy or dc:
                remote(Z.at[core], G.at[mine], sg, rg, chip * 2 + core, (yy + dy) % NY).start()
    G[mine] = Z[c]
    gathered = remote(G.at[pl.ds(0, 7)], G.at[pl.ds(0, 7)], sg, rg, mate)
    gathered.wait_recv()

    held = G[...]
    period = jnp.concatenate([held, pltpu.roll(held, 64, 2)], axis=1).reshape(256, 128)
    curved = pltpu.roll(period, 255, 0) - 2.0 * period + pltpu.roll(period, 1, 0)
    lane = lax.broadcasted_iota(jnp.int32, (8, 128), 1)
    own_half = jnp.where((lane // 32) % 2 == c, lag_ref[...], lag2[...])
    lags = jnp.where(lane // 64 == c, own_half, 0)
    lags = lags + pltpu.roll(lags, 64, 1)
    lags = ((lags + 256 - yy * 64) % 256)[0:1, :]
    shifted = curved
    for bit in range(8):
        chosen = jnp.broadcast_to((lags // (1 << bit)) % 2 == 1, (256, 128))
        shifted = jnp.where(chosen, pltpu.roll(shifted, 1 << bit, 0), shifted)
    slab = shifted[0:64, :]
    slab = slab + pltpu.roll(slab, 96, 1)
    M[...] = jnp.transpose(jnp.concatenate([slab, slab], axis=0))
    for i in range(32):
        HS[i] = M[pl.ds(i, 1), :]

    def m_h(r):
        to = dev(r // NZ, r % NZ, c)
        return remote(HS.at[to // 2], HR.at[r - 1], sh, rh, to)

    def send(r, carry):
        m_h(r).start()
        return carry

    lax.fori_loop(1, 32, send, 0)

    wait_all = [core_copy(i, j) for i in range(NX) for j in range(NZ)]
    wait_all += [m_a1(d, j) for d in range(2) for j in range(NZ)]
    wait_all += [m_a2(d, j) for d in range(2) for j in range(NZ)]
    wait_all += [m_a3(d) for d in range(2)]
    wait_all += [m_a4(d, k) for d in range(2) for k in range(3)]
    wait_all += [m_b1(d, i) for d in range(2) for i in range(NX)]
    wait_all += [m_b2(d, k, i) for d in range(2) for k in range(3) for i in range(NX)]
    wait_all += [m_b3(d) for d in range(2)]
    wait_all += [m_b4(d) for d in range(2)]
    gathered.wait_send()
    for copy in wait_all:
        copy.wait_send()

    own = HS[chip]
    scattered = remote(HS.at[pl.ds(0, 31)], HR.at[pl.ds(0, 31)], sh, rh, mate)
    scattered.wait_send()
    scattered.wait_recv()
    total = own + jnp.sum(HR[...], axis=0)
    out_ref[...] = total[:, 0:64]


def body(density, flow_rest, dest, weights, directions, bins):
    f32, bf16 = jnp.float32, jnp.bfloat16
    vm, dma = pltpu.VMEM, pltpu.SemaphoreType.DMA
    tile = (16, 128)
    scratch = [
        vm((ROWS_DEV + 1, 64, 128), bf16),
        vm((ROWS_DEV + 1, 4, 64, 128), bf16),
        vm((64, 128), jnp.int32),
        pltpu.SMEM((64, 128), jnp.int32),
        vm((8, 128), jnp.int32),
        vm((NX, NZ, 24) + tile, f32),
        vm((NX, NZ, 24) + tile, f32),
        vm((NX, NZ, 24) + tile, f32),
        vm((2, NZ, NA) + tile, f32),
        vm((2, NZ, 2 * NA) + tile, f32),
        vm((2, NA) + tile, f32),
        vm((2, 3, 2 * NA) + tile, f32),
        vm((2, NX, NB) + tile, f32),
        vm((2, 3, NX, 2 * NB) + tile, f32),
        vm((2, NB) + tile, f32),
        vm((2, 2 * NB) + tile, f32),
        vm((2, 64, 32, 128), bf16),
        vm((8, 128), jnp.int32),
        vm((2,) + tile, f32),
        vm((8,) + tile, f32),
        vm((128, 128), f32),
        vm((32, 1, 128), f32),
        vm((31, 1, 128), f32),
        dma((4,)),
    ]
    for shape in ((NX, NZ), (2, NZ), (2, NZ), (2,), (2, 3), (2, NX), (2, 3, NX), (2,), (2,)):
        scratch += [dma(shape), dma(shape)]
    scratch += [dma(())] * 8 + [pltpu.SemaphoreType.REGULAR] * 2
    return pl.pallas_call(
        main_kernel,
        out_shape=jax.ShapeDtypeStruct((1, 64), f32),
        in_specs=[
            pl.BlockSpec(memory_space=pltpu.SMEM),
            pl.BlockSpec(memory_space=pltpu.VMEM),
            pl.BlockSpec(memory_space=pltpu.VMEM),
            pl.BlockSpec(memory_space=pl.ANY),
            pl.BlockSpec(memory_space=pl.ANY),
            pl.BlockSpec(memory_space=pl.ANY),
        ],
        out_specs=pl.BlockSpec(memory_space=pltpu.VMEM),
        scratch_shapes=scratch,
        compiler_params=pltpu.CompilerParams(
            collective_id=0, has_side_effects=True, vmem_limit_bytes=60 << 20
        ),
        name="rotor",
    )(directions.T, dest.T, bins.T, density, flow_rest, weights)


def solution(mesh):
    placed = (
        P("blk", "tm", None),
        P("blk", None, "tm", None),
        P("blk", None),
        P("blk", None, "tm", None),
        P(),
        P(None, "blk"),
    )
    return jax.shard_map(
        body, mesh=mesh, in_specs=placed, out_specs=P("blk", "tm"), check_vma=False
    )
```

```python
import jax
import jax.numpy as jnp
from jax import lax
from jax.experimental import pallas as pl
from jax.experimental.pallas import tpu as pltpu
from jax.sharding import PartitionSpec as P

NX, NZ, NY = 4, 8, 4
ROWS_DEV = 96
SLOTS = 4
NA = 8
NB = 12 - NA
TILES = [(0, i) for i in range(6)] + [(1, i) for i in (5, 4, 3, 2, 1, 0)]
A0, A1, A2 = 0, NA, 2 * NA
B0, B1, B2 = 2 * NA, 2 * NA + NB, 2 * NA + 2 * NB
MESH = pl.DeviceIdType.MESH
STEPS = 32512.0


def place(j, tile):
    if tile < NA:
        return j * NA + tile
    return 2 * NA + j * NB + tile - NA


def far_first(i, n):
    step = (i + 1) // 2
    return (n // 2 + step * (1 - 2 * (i % 2))) % n


def encode(x0, x1):
    parts, steps = [], []
    for x in (x0, x1):
        hi = x.astype(jnp.bfloat16)
        wide = hi.astype(jnp.float32)
        ratio = (x - wide) / jnp.where(wide == 0.0, 1.0, wide)
        parts.append(hi)
        steps.append((ratio * STEPS + 128.5).astype(jnp.int32))
    return parts[0], parts[1], ((steps[0] - 128) * 256 + steps[1]).astype(jnp.int16)


def decode(hi0, hi1, low):
    low = low.astype(jnp.int32)
    out = []
    for hi, step in ((hi0, low >> 8), (hi1, (low & 255) - 128)):
        out.append(hi.astype(jnp.float32) * (1.0 + step.astype(jnp.float32) * (1.0 / STEPS)))
    return out


def main_kernel(
    dir_hbm, dest_hbm, bins_hbm, dens_hbm, flow_hbm, wts_hbm, out_ref,
    dir_ref, dest_ref, bins_ref, dens, flow, list_vm, list_ref, lag_ref, C, S, R0, HC, LC, RA1, LA1, RA2, LA2, RA3, LA3, RA4, LA4,
    RB1, LB1, RB2, LB2, RB3, LB3, RB4, LB4, W, lag2, Z, G, M, HS, HR,
    ld_sem, s0, r0, sa1, ra1, sa2, ra2, sa3, ra3, sa4, ra4,
    sb1, rb1, sb2, rb2, sb3, rb3, sb4, rb4, sw, rw, sl, rl, sg, rg, sh, rh, met_y, met_mate,
):
    blk = lax.axis_index("blk")
    yy = lax.axis_index("tm")
    c = blk % 2
    chip = blk // 2
    z = chip % NZ
    x = chip // NZ

    def dev(dx, dz, core):
        return (((x + dx) % NX) * NZ + (z + dz) % NZ) * 2 + core

    near_x = (dev(1, 0, c), dev(NX - 1, 0, c))
    near_z = (dev(0, 1, c), dev(0, NZ - 1, c))
    mate = dev(0, 0, 1 - c)

    def remote(src, dst, ssem, rsem, to, ty=None):
        return pltpu.make_async_remote_copy(
            src_ref=src, dst_ref=dst, send_sem=ssem, recv_sem=rsem,
            device_id=(to, yy if ty is None else ty), device_id_type=MESH,
        )

    barrier = pltpu.get_barrier_semaphore()
    along_y = ((yy + 1) % NY, (yy + NY - 1) % NY)
    for to in near_x + near_z + (mate,):
        pl.semaphore_signal(barrier, inc=1, device_id=(to, yy), device_id_type=MESH)
    for to in along_y:
        pl.semaphore_signal(barrier, inc=1, device_id=(blk, to), device_id_type=MESH)

    small = [
        pltpu.make_async_copy(dest_hbm, dest_ref, ld_sem.at[4]),
        pltpu.make_async_copy(bins_hbm, bins_ref, ld_sem.at[5]),
        pltpu.make_async_copy(dir_hbm, dir_ref, ld_sem.at[6]),
    ]
    loads = [
        pltpu.make_async_copy(dens_hbm, dens.at[pl.ds(0, ROWS_DEV)], ld_sem.at[0]),
        pltpu.make_async_copy(flow_hbm, flow.at[pl.ds(0, ROWS_DEV)], ld_sem.at[1]),
        pltpu.make_async_copy(
            wts_hbm.at[0, :, pl.ds(pl.multiple_of(c * 32, 32), 32), :], W.at[c], ld_sem.at[2]
        ),
    ]
    for copy in small + loads:
        copy.start()
    small[0].wait()
    small[1].wait()

    target = jnp.broadcast_to(dest_ref[...], (64, ROWS_DEV))
    hit = target == lax.broadcasted_iota(jnp.int32, (64, ROWS_DEV), 0)
    earlier = lax.broadcasted_iota(jnp.int32, (ROWS_DEV, ROWS_DEV), 0) < lax.broadcasted_iota(
        jnp.int32, (ROWS_DEV, ROWS_DEV), 1
    )

    def exact(flags):
        return jnp.where(flags, 1.0, 0.0).astype(jnp.bfloat16)

    before = jnp.dot(exact(hit), exact(earlier), preferred_element_type=jnp.float32)
    lane96 = lax.broadcasted_iota(jnp.int32, (ROWS_DEV, 128), 1)
    number = lax.broadcasted_iota(jnp.int32, (ROWS_DEV, 128), 0) - ROWS_DEV
    lists = jnp.full((64, 128), float(ROWS_DEV), jnp.float32)
    for s in range(SLOTS):
        column = jnp.where(lane96 == s, number, 0).astype(jnp.float32).astype(jnp.bfloat16)
        lists = lists + jnp.dot(
            exact(hit & (before == float(s))), column, preferred_element_type=jnp.float32
        )
    lists = jnp.clip(lists.astype(jnp.int32), 0, ROWS_DEV)
    lane64 = lax.broadcasted_iota(jnp.int32, (64, 128), 1)
    list_vm[...] = lists
    list_copy = pltpu.make_async_copy(list_vm, list_ref, ld_sem.at[3])
    list_copy.start()

    source = lax.broadcasted_iota(jnp.int32, (64, 128), 0)
    wanted = 2 * (lane64 % 32) + lane64 // 64
    spread = exact(source == wanted)
    lag_ref[...] = jnp.dot(
        jnp.broadcast_to(bins_ref[...], (8, 64)).astype(jnp.float32).astype(jnp.bfloat16),
        spread,
        preferred_element_type=jnp.float32,
    ).astype(jnp.int32)

    dens[ROWS_DEV] = jnp.zeros((64, 128), jnp.bfloat16)
    flow[ROWS_DEV] = jnp.zeros((4, 64, 128), jnp.bfloat16)

    pl.semaphore_wait(barrier, 7)
    for to in along_y:
        pl.semaphore_signal(met_y, inc=1, device_id=(blk, to), device_id_type=MESH)

    wts_copy = remote(
        wts_hbm.at[0, :, pl.ds(pl.multiple_of((1 - c) * 32, 32), 32), :], W.at[c], sw, rw, mate
    )
    lag_copy = remote(lag_ref, lag2, sl, rl, mate)

    list_copy.wait()
    loads[0].wait()
    loads[1].wait()

    def core_copy(dx, dz):
        return remote(S.at[dx, dz], R0.at[dx, dz], s0.at[dx, dz], r0.at[dx, dz], mate)

    def unit(dx, dz):
        first = dev(dx, dz, 0)
        for j in range(2):
            rows = [list_ref[first + j, s] for s in range(SLOTS)]
            for part in range(2):
                target = C if part == 0 else S
                for chunk in range(2):
                    off = pl.multiple_of(((c + part) % 2) * 32 + chunk * 16, 16)
                    span = pl.ds(off, 16)
                    acc = None
                    for r in rows:
                        rho = dens[r, span, :].astype(jnp.float32)
                        u = flow[r, 0, span, :].astype(jnp.float32)
                        v = flow[r, 1, span, :].astype(jnp.float32)
                        w = flow[r, 2, span, :].astype(jnp.float32)
                        e = flow[r, 3, span, :].astype(jnp.float32)
                        ru, rv, rw_ = rho * u, rho * v, rho * w
                        terms = [ru * u, rv * v, rw_ * w, ru * v, ru * w, rv * w, e]
                        acc = terms if acc is None else [p + q for p, q in zip(acc, terms)]
                    sums = [acc[0] + acc[6], acc[1] + acc[6], acc[2] + acc[6], acc[3], acc[4], acc[5]]
                    for tile, (ch, comp) in enumerate(TILES):
                        if ch == chunk:
                            target[dx, dz, place(j, tile)] = sums[comp]
        core_copy(dx, dz).start()

    def combine(dx, dz, spans, send):
        for lo, hi, came in spans:

            def pair(p, carry):
                t = lo + 2 * p
                sums = [C[dx, dz, t], C[dx, dz, t + 1]]
                for hi_ref, low_ref, start in came:
                    k = t - start
                    more = decode(hi_ref[k], hi_ref[k + 1], low_ref[(lo - start) // 2 + p])
                    sums = [q + r for q, r in zip(sums, more)]
                if send:
                    h0, h1, low = encode(*sums)
                    HC[dx, dz, t] = h0
                    HC[dx, dz, t + 1] = h1
                    LC[dx, dz, lo // 2 + p] = low
                else:
                    C[dx, dz, t] = sums[0]
                    C[dx, dz, t + 1] = sums[1]
                return carry

            lax.fori_loop(0, (hi - lo) // 2, pair, 0, unroll=4)

    half_a = ((A0, A1), (A1, A2))
    half_b = ((B0, B1), (B1, B2))

    class Message:
        def __init__(self, dx, dz, span, hi_ref, low_ref, ssem, rsem, to):
            lo, n = span[0], span[1] - span[0]
            self.copies = [
                remote(HC.at[dx, dz, pl.ds(lo, n)], hi_ref, ssem(0), rsem(0), to),
                remote(LC.at[dx, dz, pl.ds(lo // 2, n // 2)], low_ref, ssem(1), rsem(1), to),
            ]
            self.came = (hi_ref, low_ref, lo)

        def start(self):
            for copy in self.copies:
                copy.start()

        def wait_send(self):
            for copy in self.copies:
                copy.wait_send()

        def wait_recv(self):
            for copy in self.copies:
                copy.wait_recv()
            return self.came

    def message(dx, dz, span, hi_ref, low_ref, ssem, rsem, to, *at):
        return Message(
            dx, dz, span, hi_ref.at[at], low_ref.at[at],
            lambda i: ssem.at[at + (i,)], lambda i: rsem.at[at + (i,)], to,
        )

    def m_a1(d, dz):
        return message(2, dz, half_a[d], RA1, LA1, sa1, ra1, near_x[d], d, dz)

    def m_a2(d, dz):
        return message(1 if d == 0 else 3, dz, (A0, A2), RA2, LA2, sa2, ra2, near_x[d], d, dz)

    def m_a3(d):
        return message(0, 4, half_a[d], RA3, LA3, sa3, ra3, near_z[d], d)

    def m_a4(d, k):
        dz = 3 - k if d == 0 else 5 + k
        return message(0, dz, (A0, A2), RA4, LA4, sa4, ra4, near_z[d], d, k)

    def m_b1(d, dx):
        return message(dx, 4, half_b[d], RB1, LB1, sb1, rb1, near_z[d], d, dx)

    def m_b2(d, k, dx):
        dz = 3 - k if d == 0 else 5 + k
        return message(dx, dz, (B0, B2), RB2, LB2, sb2, rb2, near_z[d], d, k, dx)

    def m_b3(d):
        return message(2, 0, half_b[d], RB3, LB3, sb3, rb3, near_x[d], d)

    def m_b4(d):
        return message(1 if d == 0 else 3, 0, (B0, B2), RB4, LB4, sb4, rb4, near_x[d], d)

    def halves(pair, d, extra, both=()):
        return [(lo, hi, list(both) + ([extra] if i == d else [])) for i, (lo, hi) in enumerate(pair)]

    def finish(gp):
        dz = far_first(gp, NZ)

        def step(k, carry):
            dx = far_first(k, NX)
            core_copy(dx, dz).wait_recv()
            C[dx, dz] = C[dx, dz] + R0[dx, dz]

            @pl.when(k == 0)
            def _():
                for d in range(2):
                    combine(2, dz, [half_a[d] + ((),)], True)
                    m_a1(d, dz).start()

            @pl.when(gp == 0)
            def _():
                for d in range(2):
                    combine(dx, 4, [half_b[d] + ((),)], True)
                    m_b1(d, dx).start()

            return carry

        lax.fori_loop(0, NX, step, 0)

    def ev_a2(dz):
        for d in range(2):
            came = m_a1(d, dz).wait_recv()
            combine(1 if d == 0 else 3, dz, halves(half_a, d, came), True)
            m_a2(d, dz).start()

    def ev_b2(k, dx):
        for d in range(2):
            dz = 3 - k if d == 0 else 5 + k
            if k == 0:
                spans = halves(half_b, d, m_b1(d, dx).wait_recv())
            else:
                spans = [(B0, B2, [m_b2(d, k - 1, dx).wait_recv()])]
            combine(dx, dz, spans, True)
            m_b2(d, k, dx).start()

    def ev_ra2(dz):
        both = [m_a2(0, dz).wait_recv(), m_a2(1, dz).wait_recv()]
        if dz == 4:
            combine(0, 4, [(A0, A2, both)], True)
            m_a3(0).start()
            m_a3(1).start()
        elif dz == 0:
            both += [m_a4(0, 2).wait_recv(), m_a4(1, 2).wait_recv()]
            combine(0, 0, [(A0, A2, both)], False)
        else:
            d, k = (0, 3 - dz) if dz < 4 else (1, dz - 5)
            if k == 0:
                spans = halves(half_a, d, m_a3(d).wait_recv(), both)
            else:
                spans = [(A0, A2, both + [m_a4(d, k - 1).wait_recv()])]
            combine(0, dz, spans, True)
            m_a4(d, k).start()

    def ev_rb2(dx):
        both = [m_b2(0, 2, dx).wait_recv(), m_b2(1, 2, dx).wait_recv()]
        if dx == 2:
            combine(2, 0, [(B0, B2, both)], True)
            m_b3(0).start()
            m_b3(1).start()
        elif dx == 0:
            both += [m_b4(0).wait_recv(), m_b4(1).wait_recv()]
            combine(0, 0, [(B0, B2, both)], False)
        else:
            d = 0 if dx == 1 else 1
            combine(dx, 0, halves(half_b, d, m_b3(d).wait_recv(), both), True)
            m_b4(d).start()

    def group(g, carry):
        dz = far_first(g, NZ)

        def step(k, inner):
            unit(far_first(k, NX), dz)
            return inner

        lax.fori_loop(0, NX, step, 0)

        @pl.when(g >= 1)
        def _():
            finish(g - 1)

        @pl.when(g == 3)
        def _():
            def send(k, inner):
                ev_b2(0, far_first(k, NX))
                return inner

            lax.fori_loop(0, NX, send, 0)

        @pl.when(g >= 4)
        def _():
            ev_a2(far_first(g - 4, NZ))

        return carry

    lax.fori_loop(0, NZ, group, 0)
    wts_copy.start()
    lag_copy.start()
    pl.semaphore_wait(met_y, 2)
    pl.semaphore_signal(met_mate, inc=1, device_id=(mate, yy), device_id_type=MESH)
    finish(NZ - 1)
    ev_b2(1, 2)
    ev_b2(1, 1)
    ev_b2(1, 3)
    ev_a2(6)
    ev_b2(1, 0)
    ev_a2(1)
    ev_b2(2, 2)
    ev_ra2(4)
    ev_b2(2, 1)
    ev_ra2(3)
    ev_b2(2, 3)
    ev_b2(2, 0)
    ev_ra2(5)
    ev_rb2(2)
    ev_a2(7)
    ev_a2(0)
    ev_ra2(2)
    ev_ra2(6)
    ev_ra2(1)
    ev_rb2(1)
    ev_rb2(3)
    ev_ra2(7)
    ev_ra2(0)
    ev_rb2(0)

    loads[2].wait()
    small[2].wait()
    wts_copy.wait()
    lag_copy.wait()
    lane16 = lax.broadcasted_iota(jnp.int32, (16, 128), 1)

    def project(o, carry):
        d0, d1, d2 = dir_ref[0, o], dir_ref[1, o], dir_ref[2, o]
        coef = [d0 * d0, d1 * d1, d2 * d2, 2.0 * d0 * d1, 2.0 * d0 * d2, 2.0 * d1 * d2]
        new = []
        for chunk in range(2):
            out = carry[chunk]
            for j in range(2):
                moment = None
                for tile, (ch, comp) in enumerate(TILES):
                    if ch == chunk:
                        term = coef[comp] * C[0, 0, place(j, tile)]
                        moment = term if moment is None else moment + term
                weight = W[j, o, pl.ds(chunk * 16, 16), :].astype(jnp.float32)
                value = jnp.sum(weight * moment, axis=1, keepdims=True)
                out = jnp.where(lane16 == (o % 2) * 64 + j * 32 + o // 2, value, out)
            new.append(out)
        return tuple(new)

    zero = jnp.zeros((16, 128), jnp.float32)
    cols = lax.fori_loop(0, 64, project, (zero, zero), unroll=8)

    low = lane16 < 64
    Z[0] = jnp.where(low, cols[0], pltpu.roll(cols[1], 64, 1))
    Z[1] = jnp.where(low, pltpu.roll(cols[0], 64, 1), cols[1])
    pl.semaphore_wait(met_mate, 1)
    mine = yy * 2 + c
    for dc in range(2):
        for dy in range(NY):
            core = (c + dc) % 2
            if dy or dc:
                remote(Z.at[core], G.at[mine], sg, rg, chip * 2 + core, (yy + dy) % NY).start()
    G[mine] = Z[c]
    gathered = remote(G.at[pl.ds(0, 7)], G.at[pl.ds(0, 7)], sg, rg, mate)
    gathered.wait_recv()

    held = G[...]
    period = jnp.concatenate([held, pltpu.roll(held, 64, 2)], axis=1).reshape(256, 128)
    curved = pltpu.roll(period, 255, 0) - 2.0 * period + pltpu.roll(period, 1, 0)
    lane = lax.broadcasted_iota(jnp.int32, (8, 128), 1)
    own_half = jnp.where((lane // 32) % 2 == c, lag_ref[...], lag2[...])
    lags = jnp.where(lane // 64 == c, own_half, 0)
    lags = lags + pltpu.roll(lags, 64, 1)
    lags = ((lags + 256 - yy * 64) % 256)[0:1, :]
    shifted = curved
    for bit in range(8):
        chosen = jnp.broadcast_to((lags // (1 << bit)) % 2 == 1, (256, 128))
        shifted = jnp.where(chosen, pltpu.roll(shifted, 1 << bit, 0), shifted)
    slab = shifted[0:64, :]
    slab = slab + pltpu.roll(slab, 96, 1)
    M[...] = jnp.transpose(jnp.concatenate([slab, slab], axis=0))
    for i in range(32):
        HS[i] = M[pl.ds(i, 1), :]

    def m_h(r):
        to = dev(r // NZ, r % NZ, c)
        return remote(HS.at[to // 2], HR.at[r - 1], sh, rh, to)

    def send(r, carry):
        m_h(r).start()
        return carry

    lax.fori_loop(1, 32, send, 0)

    wait_all = [core_copy(i, j) for i in range(NX) for j in range(NZ)]
    wait_all += [m_a1(d, j) for d in range(2) for j in range(NZ)]
    wait_all += [m_a2(d, j) for d in range(2) for j in range(NZ)]
    wait_all += [m_a3(d) for d in range(2)]
    wait_all += [m_a4(d, k) for d in range(2) for k in range(3)]
    wait_all += [m_b1(d, i) for d in range(2) for i in range(NX)]
    wait_all += [m_b2(d, k, i) for d in range(2) for k in range(3) for i in range(NX)]
    wait_all += [m_b3(d) for d in range(2)]
    wait_all += [m_b4(d) for d in range(2)]
    gathered.wait_send()
    for copy in wait_all:
        copy.wait_send()

    own = HS[chip]
    scattered = remote(HS.at[pl.ds(0, 31)], HR.at[pl.ds(0, 31)], sh, rh, mate)
    scattered.wait_send()
    scattered.wait_recv()
    total = own + jnp.sum(HR[...], axis=0)
    out_ref[...] = total[:, 0:64]


def body(density, flow_rest, dest, weights, directions, bins):
    f32, bf16 = jnp.float32, jnp.bfloat16
    vm, dma = pltpu.VMEM, pltpu.SemaphoreType.DMA
    tile = (16, 128)
    scratch = [
        pltpu.SMEM((3, 64), f32),
        vm((1, ROWS_DEV), jnp.int32),
        vm((1, 64), jnp.int32),
        vm((ROWS_DEV + 1, 64, 128), bf16),
        vm((ROWS_DEV + 1, 4, 64, 128), bf16),
        vm((64, 128), jnp.int32),
        pltpu.SMEM((64, 128), jnp.int32),
        vm((8, 128), jnp.int32),
        vm((NX, NZ, 24) + tile, f32),
        vm((NX, NZ, 24) + tile, f32),
        vm((NX, NZ, 24) + tile, f32),
        vm((NX, NZ, 24) + tile, bf16),
        vm((NX, NZ, 12) + tile, jnp.int16),
    ]
    for shape, n in (
        ((2, NZ), NA), ((2, NZ), 2 * NA), ((2,), NA), ((2, 3), 2 * NA),
        ((2, NX), NB), ((2, 3, NX), 2 * NB), ((2,), NB), ((2,), 2 * NB),
    ):
        scratch += [vm(shape + (n,) + tile, bf16), vm(shape + (n // 2,) + tile, jnp.int16)]
    scratch += [
        vm((2, 64, 32, 128), bf16),
        vm((8, 128), jnp.int32),
        vm((2,) + tile, f32),
        vm((8,) + tile, f32),
        vm((128, 128), f32),
        vm((32, 1, 128), f32),
        vm((31, 1, 128), f32),
        dma((7,)),
    ]
    scratch += [dma((NX, NZ))] * 2
    for shape in ((2, NZ), (2, NZ), (2,), (2, 3), (2, NX), (2, 3, NX), (2,), (2,)):
        scratch += [dma(shape + (2,))] * 2
    scratch += [dma(())] * 8 + [pltpu.SemaphoreType.REGULAR] * 2
    return pl.pallas_call(
        main_kernel,
        out_shape=jax.ShapeDtypeStruct((1, 64), f32),
        in_specs=[
            pl.BlockSpec(memory_space=pl.ANY)
        ] * 6,
        out_specs=pl.BlockSpec(memory_space=pltpu.VMEM),
        scratch_shapes=scratch,
        compiler_params=pltpu.CompilerParams(
            collective_id=0, has_side_effects=True, vmem_limit_bytes=60 << 20
        ),
        name="rotor",
    )(directions.T, dest.T, bins.T, density, flow_rest, weights)


def solution(mesh):
    placed = (
        P("blk", "tm", None),
        P("blk", None, "tm", None),
        P("blk", None),
        P("blk", None, "tm", None),
        P(),
        P(None, "blk"),
    )
    return jax.shard_map(
        body, mesh=mesh, in_specs=placed, out_specs=P("blk", "tm"), check_vma=False
    )
```

```python
import jax
import jax.numpy as jnp
from jax import lax
from jax.experimental import pallas as pl
from jax.experimental.pallas import tpu as pltpu
from jax.sharding import PartitionSpec as P

NX, NZ, NY = 4, 8, 4
ROWS_DEV = 96
SLOTS = 4
NA = 8
NB = 12 - NA
TILES = [(0, i) for i in range(6)] + [(1, i) for i in (5, 4, 3, 2, 1, 0)]
A0, A1, A2 = 0, NA, 2 * NA
B0, B1, B2 = 2 * NA, 2 * NA + NB, 2 * NA + 2 * NB
MESH = pl.DeviceIdType.MESH
STEPS = 32512.0


def place(j, tile):
    if tile < NA:
        return j * NA + tile
    return 2 * NA + j * NB + tile - NA


def far_first(i, n):
    step = (i + 1) // 2
    return (n // 2 + step * (1 - 2 * (i % 2))) % n


def encode(x0, x1):
    parts, steps = [], []
    for x in (x0, x1):
        hi = x.astype(jnp.bfloat16)
        wide = hi.astype(jnp.float32)
        ratio = (x - wide) / jnp.where(wide == 0.0, 1.0, wide)
        parts.append(hi)
        steps.append((ratio * STEPS + 128.5).astype(jnp.int32))
    return parts[0], parts[1], ((steps[0] - 128) * 256 + steps[1]).astype(jnp.int16)


def decode(hi0, hi1, low):
    low = low.astype(jnp.int32)
    out = []
    for hi, step in ((hi0, low >> 8), (hi1, (low & 255) - 128)):
        out.append(hi.astype(jnp.float32) * (1.0 + step.astype(jnp.float32) * (1.0 / STEPS)))
    return out


def main_kernel(
    dir_hbm, dest_hbm, bins_hbm, dens_hbm, flow_hbm, wts_hbm, out_ref,
    dir_ref, dest_ref, bins_ref, dens_own, flow_own, dens_mate, flow_mate, list_vm, list_ref, lag_ref, C, S, R0, HC, LC, RA1, LA1, RA2, LA2, RA3, LA3, RA4, LA4,
    RB1, LB1, RB2, LB2, RB3, LB3, RB4, LB4, W, lag2, Z, G, M, HS, HR,
    ld_sem, s0, r0, sa1, ra1, sa2, ra2, sa3, ra3, sa4, ra4,
    sb1, rb1, sb2, rb2, sb3, rb3, sb4, rb4, sw, rw, sl, rl, sg, rg, sh, rh, met_y, met_mate,
):
    blk = lax.axis_index("blk")
    yy = lax.axis_index("tm")
    c = blk % 2
    chip = blk // 2
    z = chip % NZ
    x = chip // NZ

    def dev(dx, dz, core):
        return (((x + dx) % NX) * NZ + (z + dz) % NZ) * 2 + core

    near_x = (dev(1, 0, c), dev(NX - 1, 0, c))
    near_z = (dev(0, 1, c), dev(0, NZ - 1, c))
    mate = dev(0, 0, 1 - c)

    def remote(src, dst, ssem, rsem, to, ty=None):
        return pltpu.make_async_remote_copy(
            src_ref=src, dst_ref=dst, send_sem=ssem, recv_sem=rsem,
            device_id=(to, yy if ty is None else ty), device_id_type=MESH,
        )

    barrier = pltpu.get_barrier_semaphore()
    along_y = ((yy + 1) % NY, (yy + NY - 1) % NY)
    for to in near_x + near_z + (mate,):
        pl.semaphore_signal(barrier, inc=1, device_id=(to, yy), device_id_type=MESH)
    for to in along_y:
        pl.semaphore_signal(barrier, inc=1, device_id=(blk, to), device_id_type=MESH)

    small = [
        pltpu.make_async_copy(dest_hbm, dest_ref, ld_sem.at[4]),
        pltpu.make_async_copy(bins_hbm, bins_ref, ld_sem.at[5]),
        pltpu.make_async_copy(dir_hbm, dir_ref, ld_sem.at[6]),
    ]
    def half(core):
        return pl.ds(pl.multiple_of(core * 32, 32), 32)

    def row_loads(core, dens, flow, at):
        rows = pl.ds(0, ROWS_DEV)
        return [
            pltpu.make_async_copy(dens_hbm.at[:, half(core), :], dens.at[rows], ld_sem.at[at]),
            pltpu.make_async_copy(flow_hbm.at[:, :, half(core), :], flow.at[rows], ld_sem.at[at + 1]),
        ]

    loads_mate = row_loads(1 - c, dens_mate, flow_mate, 0)
    loads_own = row_loads(c, dens_own, flow_own, 7)
    own_wts = pltpu.make_async_copy(wts_hbm.at[0, :, half(c), :], W.at[c], ld_sem.at[2])
    for copy in small + loads_mate + loads_own + [own_wts]:
        copy.start()
    small[0].wait()
    small[1].wait()

    target = jnp.broadcast_to(dest_ref[...], (64, ROWS_DEV))
    hit = target == lax.broadcasted_iota(jnp.int32, (64, ROWS_DEV), 0)
    earlier = lax.broadcasted_iota(jnp.int32, (ROWS_DEV, ROWS_DEV), 0) < lax.broadcasted_iota(
        jnp.int32, (ROWS_DEV, ROWS_DEV), 1
    )

    def exact(flags):
        return jnp.where(flags, 1.0, 0.0).astype(jnp.bfloat16)

    before = jnp.dot(exact(hit), exact(earlier), preferred_element_type=jnp.float32)
    lane96 = lax.broadcasted_iota(jnp.int32, (ROWS_DEV, 128), 1)
    number = lax.broadcasted_iota(jnp.int32, (ROWS_DEV, 128), 0) - ROWS_DEV
    lists = jnp.full((64, 128), float(ROWS_DEV), jnp.float32)
    for s in range(SLOTS):
        column = jnp.where(lane96 == s, number, 0).astype(jnp.float32).astype(jnp.bfloat16)
        lists = lists + jnp.dot(
            exact(hit & (before == float(s))), column, preferred_element_type=jnp.float32
        )
    lists = jnp.clip(lists.astype(jnp.int32), 0, ROWS_DEV)
    lane64 = lax.broadcasted_iota(jnp.int32, (64, 128), 1)
    list_vm[...] = lists
    list_copy = pltpu.make_async_copy(list_vm, list_ref, ld_sem.at[3])
    list_copy.start()

    source = lax.broadcasted_iota(jnp.int32, (64, 128), 0)
    wanted = 2 * (lane64 % 32) + lane64 // 64
    spread = exact(source == wanted)
    lag_ref[...] = jnp.dot(
        jnp.broadcast_to(bins_ref[...], (8, 64)).astype(jnp.float32).astype(jnp.bfloat16),
        spread,
        preferred_element_type=jnp.float32,
    ).astype(jnp.int32)

    for dens, flow in ((dens_own, flow_own), (dens_mate, flow_mate)):
        dens[ROWS_DEV] = jnp.zeros((32, 128), jnp.bfloat16)
        flow[ROWS_DEV] = jnp.zeros((4, 32, 128), jnp.bfloat16)

    pl.semaphore_wait(barrier, 7)
    for to in along_y:
        pl.semaphore_signal(met_y, inc=1, device_id=(blk, to), device_id_type=MESH)

    wts_copy = remote(
        wts_hbm.at[0, :, pl.ds(pl.multiple_of((1 - c) * 32, 32), 32), :], W.at[c], sw, rw, mate
    )
    lag_copy = remote(lag_ref, lag2, sl, rl, mate)

    list_copy.wait()
    for copy in loads_mate:
        copy.wait()

    def core_copy(dx, dz):
        return remote(S.at[dx, dz], R0.at[dx, dz], s0.at[dx, dz], r0.at[dx, dz], mate)

    def unit(dx, dz, part):
        first = dev(dx, dz, 0)
        target = C if part == 0 else S
        dens, flow = (dens_own, flow_own) if part == 0 else (dens_mate, flow_mate)
        for j in range(2):
            rows = [list_ref[first + j, s] for s in range(SLOTS)]
            for chunk in range(2):
                span = pl.ds(chunk * 16, 16)
                acc = None
                for r in rows:
                    rho = dens[r, span, :].astype(jnp.float32)
                    u = flow[r, 0, span, :].astype(jnp.float32)
                    v = flow[r, 1, span, :].astype(jnp.float32)
                    w = flow[r, 2, span, :].astype(jnp.float32)
                    e = flow[r, 3, span, :].astype(jnp.float32)
                    ru, rv, rw_ = rho * u, rho * v, rho * w
                    terms = [ru * u, rv * v, rw_ * w, ru * v, ru * w, rv * w, e]
                    acc = terms if acc is None else [p + q for p, q in zip(acc, terms)]
                sums = [acc[0] + acc[6], acc[1] + acc[6], acc[2] + acc[6], acc[3], acc[4], acc[5]]
                for tile, (ch, comp) in enumerate(TILES):
                    if ch == chunk:
                        target[dx, dz, place(j, tile)] = sums[comp]
        if part == 1:
            core_copy(dx, dz).start()

    def combine(dx, dz, spans, send):
        for lo, hi, came in spans:

            def pair(p, carry):
                t = lo + 2 * p
                sums = [C[dx, dz, t], C[dx, dz, t + 1]]
                for hi_ref, low_ref, start in came:
                    k = t - start
                    more = decode(hi_ref[k], hi_ref[k + 1], low_ref[(lo - start) // 2 + p])
                    sums = [q + r for q, r in zip(sums, more)]
                if send:
                    h0, h1, low = encode(*sums)
                    HC[dx, dz, t] = h0
                    HC[dx, dz, t + 1] = h1
                    LC[dx, dz, lo // 2 + p] = low
                else:
                    C[dx, dz, t] = sums[0]
                    C[dx, dz, t + 1] = sums[1]
                return carry

            lax.fori_loop(0, (hi - lo) // 2, pair, 0, unroll=4)

    half_a = ((A0, A1), (A1, A2))
    half_b = ((B0, B1), (B1, B2))

    class Message:
        def __init__(self, dx, dz, span, hi_ref, low_ref, ssem, rsem, to):
            lo, n = span[0], span[1] - span[0]
            self.copies = [
                remote(HC.at[dx, dz, pl.ds(lo, n)], hi_ref, ssem(0), rsem(0), to),
                remote(LC.at[dx, dz, pl.ds(lo // 2, n // 2)], low_ref, ssem(1), rsem(1), to),
            ]
            self.came = (hi_ref, low_ref, lo)

        def start(self):
            for copy in self.copies:
                copy.start()

        def wait_send(self):
            for copy in self.copies:
                copy.wait_send()

        def wait_recv(self):
            for copy in self.copies:
                copy.wait_recv()
            return self.came

    def message(dx, dz, span, hi_ref, low_ref, ssem, rsem, to, *at):
        return Message(
            dx, dz, span, hi_ref.at[at], low_ref.at[at],
            lambda i: ssem.at[at + (i,)], lambda i: rsem.at[at + (i,)], to,
        )

    def m_a1(d, dz):
        return message(2, dz, half_a[d], RA1, LA1, sa1, ra1, near_x[d], d, dz)

    def m_a2(d, dz):
        return message(1 if d == 0 else 3, dz, (A0, A2), RA2, LA2, sa2, ra2, near_x[d], d, dz)

    def m_a3(d):
        return message(0, 4, half_a[d], RA3, LA3, sa3, ra3, near_z[d], d)

    def m_a4(d, k):
        dz = 3 - k if d == 0 else 5 + k
        return message(0, dz, (A0, A2), RA4, LA4, sa4, ra4, near_z[d], d, k)

    def m_b1(d, dx):
        return message(dx, 4, half_b[d], RB1, LB1, sb1, rb1, near_z[d], d, dx)

    def m_b2(d, k, dx):
        dz = 3 - k if d == 0 else 5 + k
        return message(dx, dz, (B0, B2), RB2, LB2, sb2, rb2, near_z[d], d, k, dx)

    def m_b3(d):
        return message(2, 0, half_b[d], RB3, LB3, sb3, rb3, near_x[d], d)

    def m_b4(d):
        return message(1 if d == 0 else 3, 0, (B0, B2), RB4, LB4, sb4, rb4, near_x[d], d)

    def halves(pair, d, extra, both=()):
        return [(lo, hi, list(both) + ([extra] if i == d else [])) for i, (lo, hi) in enumerate(pair)]

    def finish(gp):
        dz = far_first(gp, NZ)

        def step(k, carry):
            dx = far_first(k, NX)
            core_copy(dx, dz).wait_recv()
            C[dx, dz] = C[dx, dz] + R0[dx, dz]

            @pl.when(k == 0)
            def _():
                for d in range(2):
                    combine(2, dz, [half_a[d] + ((),)], True)
                    m_a1(d, dz).start()

            @pl.when(gp == 0)
            def _():
                for d in range(2):
                    combine(dx, 4, [half_b[d] + ((),)], True)
                    m_b1(d, dx).start()

            return carry

        lax.fori_loop(0, NX, step, 0)

    def ev_a2(dz):
        for d in range(2):
            came = m_a1(d, dz).wait_recv()
            combine(1 if d == 0 else 3, dz, halves(half_a, d, came), True)
            m_a2(d, dz).start()

    def ev_b2(k, dx):
        for d in range(2):
            dz = 3 - k if d == 0 else 5 + k
            if k == 0:
                spans = halves(half_b, d, m_b1(d, dx).wait_recv())
            else:
                spans = [(B0, B2, [m_b2(d, k - 1, dx).wait_recv()])]
            combine(dx, dz, spans, True)
            m_b2(d, k, dx).start()

    def ev_ra2(dz):
        both = [m_a2(0, dz).wait_recv(), m_a2(1, dz).wait_recv()]
        if dz == 4:
            combine(0, 4, [(A0, A2, both)], True)
            m_a3(0).start()
            m_a3(1).start()
        elif dz == 0:
            both += [m_a4(0, 2).wait_recv(), m_a4(1, 2).wait_recv()]
            combine(0, 0, [(A0, A2, both)], False)
        else:
            d, k = (0, 3 - dz) if dz < 4 else (1, dz - 5)
            if k == 0:
                spans = halves(half_a, d, m_a3(d).wait_recv(), both)
            else:
                spans = [(A0, A2, both + [m_a4(d, k - 1).wait_recv()])]
            combine(0, dz, spans, True)
            m_a4(d, k).start()

    def ev_rb2(dx):
        both = [m_b2(0, 2, dx).wait_recv(), m_b2(1, 2, dx).wait_recv()]
        if dx == 2:
            combine(2, 0, [(B0, B2, both)], True)
            m_b3(0).start()
            m_b3(1).start()
        elif dx == 0:
            both += [m_b4(0).wait_recv(), m_b4(1).wait_recv()]
            combine(0, 0, [(B0, B2, both)], False)
        else:
            d = 0 if dx == 1 else 1
            combine(dx, 0, halves(half_b, d, m_b3(d).wait_recv(), both), True)
            m_b4(d).start()

    def group(g, carry):
        dz = far_first(g, NZ)

        def across(k, inner):
            unit(far_first(k, NX), dz, 1)
            return inner

        def ahead(k, inner):
            unit(far_first(k, NX), far_first(g + 1, NZ), 1)
            return inner

        def own(k, inner):
            unit(far_first(k, NX), dz, 0)
            return inner

        @pl.when(g == 0)
        def _():
            lax.fori_loop(0, NX, across, 0)
            for copy in loads_own:
                copy.wait()

        @pl.when(g < NZ - 1)
        def _():
            lax.fori_loop(0, NX, ahead, 0)

        lax.fori_loop(0, NX, own, 0)

        finish(g)

        for step in range(2):

            @pl.when(g == 2 + 3 * step)
            def _(step=step):
                def send(k, inner):
                    ev_b2(step, far_first(k, NX))
                    return inner

                lax.fori_loop(0, NX, send, 0)

        @pl.when(g >= 3)
        def _():
            ev_a2(far_first(g - 3, NZ))

        return carry

    lax.fori_loop(0, NZ, group, 0)
    wts_copy.start()
    lag_copy.start()
    pl.semaphore_wait(met_y, 2)
    pl.semaphore_signal(met_mate, inc=1, device_id=(mate, yy), device_id_type=MESH)
    ev_b2(2, 2)
    ev_ra2(4)
    ev_b2(2, 1)
    ev_a2(1)
    ev_ra2(3)
    ev_b2(2, 3)
    ev_ra2(5)
    ev_b2(2, 0)
    ev_rb2(2)
    ev_a2(7)
    ev_a2(0)
    ev_ra2(2)
    ev_ra2(6)
    ev_rb2(1)
    ev_rb2(3)
    ev_ra2(1)
    ev_ra2(7)
    ev_rb2(0)
    ev_ra2(0)

    own_wts.wait()
    small[2].wait()
    wts_copy.wait()
    lag_copy.wait()
    lane16 = lax.broadcasted_iota(jnp.int32, (16, 128), 1)

    def project(o, carry):
        d0, d1, d2 = dir_ref[0, o], dir_ref[1, o], dir_ref[2, o]
        coef = [d0 * d0, d1 * d1, d2 * d2, 2.0 * d0 * d1, 2.0 * d0 * d2, 2.0 * d1 * d2]
        new = []
        for chunk in range(2):
            out = carry[chunk]
            for j in range(2):
                moment = None
                for tile, (ch, comp) in enumerate(TILES):
                    if ch == chunk:
                        term = coef[comp] * C[0, 0, place(j, tile)]
                        moment = term if moment is None else moment + term
                weight = W[j, o, pl.ds(chunk * 16, 16), :].astype(jnp.float32)
                value = jnp.sum(weight * moment, axis=1, keepdims=True)
                out = jnp.where(lane16 == (o % 2) * 64 + j * 32 + o // 2, value, out)
            new.append(out)
        return tuple(new)

    zero = jnp.zeros((16, 128), jnp.float32)
    cols = lax.fori_loop(0, 64, project, (zero, zero), unroll=8)

    low = lane16 < 64
    Z[0] = jnp.where(low, cols[0], pltpu.roll(cols[1], 64, 1))
    Z[1] = jnp.where(low, pltpu.roll(cols[0], 64, 1), cols[1])
    pl.semaphore_wait(met_mate, 1)
    mine = yy * 2 + c
    for dy in (2, 1, 3, 0):
        for dc in range(2):
            core = (c + dc) % 2
            if dy or dc:
                remote(Z.at[core], G.at[mine], sg, rg, chip * 2 + core, (yy + dy) % NY).start()
    G[mine] = Z[c]
    gathered = remote(G.at[pl.ds(0, 7)], G.at[pl.ds(0, 7)], sg, rg, mate)
    gathered.wait_recv()

    held = G[...]
    period = jnp.concatenate([held, pltpu.roll(held, 64, 2)], axis=1).reshape(256, 128)
    curved = pltpu.roll(period, 255, 0) - 2.0 * period + pltpu.roll(period, 1, 0)
    lane = lax.broadcasted_iota(jnp.int32, (8, 128), 1)
    own_half = jnp.where((lane // 32) % 2 == c, lag_ref[...], lag2[...])
    lags = jnp.where(lane // 64 == c, own_half, 0)
    lags = lags + pltpu.roll(lags, 64, 1)
    lags = ((lags + 256 - yy * 64) % 256)[0:1, :]
    shifted = curved
    for bit in range(8):
        chosen = jnp.broadcast_to((lags // (1 << bit)) % 2 == 1, (256, 128))
        shifted = jnp.where(chosen, pltpu.roll(shifted, 1 << bit, 0), shifted)
    slab = shifted[0:64, :]
    slab = slab + pltpu.roll(slab, 96, 1)
    M[...] = jnp.transpose(jnp.concatenate([slab, slab], axis=0))
    for i in range(32):
        HS[i] = M[pl.ds(i, 1), :]

    def send(i, carry):
        dx, dz = far_first(i // NZ, NX), far_first(i % NZ, NZ)
        to = dev(dx, dz, c)
        remote(HS.at[to // 2], HR.at[dx * NZ + dz - 1], sh, rh, to).start()
        return carry

    lax.fori_loop(0, NX * NZ - 1, send, 0)

    wait_all = [core_copy(i, j) for i in range(NX) for j in range(NZ)]
    wait_all += [m_a1(d, j) for d in range(2) for j in range(NZ)]
    wait_all += [m_a2(d, j) for d in range(2) for j in range(NZ)]
    wait_all += [m_a3(d) for d in range(2)]
    wait_all += [m_a4(d, k) for d in range(2) for k in range(3)]
    wait_all += [m_b1(d, i) for d in range(2) for i in range(NX)]
    wait_all += [m_b2(d, k, i) for d in range(2) for k in range(3) for i in range(NX)]
    wait_all += [m_b3(d) for d in range(2)]
    wait_all += [m_b4(d) for d in range(2)]
    gathered.wait_send()
    for copy in wait_all:
        copy.wait_send()

    own = HS[chip]
    scattered = remote(HS.at[pl.ds(0, 31)], HR.at[pl.ds(0, 31)], sh, rh, mate)
    scattered.wait_send()
    scattered.wait_recv()
    total = own + jnp.sum(HR[...], axis=0)
    out_ref[...] = total[:, 0:64]


def body(density, flow_rest, dest, weights, directions, bins):
    f32, bf16 = jnp.float32, jnp.bfloat16
    vm, dma = pltpu.VMEM, pltpu.SemaphoreType.DMA
    tile = (16, 128)
    scratch = [
        pltpu.SMEM((3, 64), f32),
        vm((1, ROWS_DEV), jnp.int32),
        vm((1, 64), jnp.int32),
        vm((ROWS_DEV + 1, 32, 128), bf16),
        vm((ROWS_DEV + 1, 4, 32, 128), bf16),
        vm((ROWS_DEV + 1, 32, 128), bf16),
        vm((ROWS_DEV + 1, 4, 32, 128), bf16),
        vm((64, 128), jnp.int32),
        pltpu.SMEM((64, 128), jnp.int32),
        vm((8, 128), jnp.int32),
        vm((NX, NZ, 24) + tile, f32),
        vm((NX, NZ, 24) + tile, f32),
        vm((NX, NZ, 24) + tile, f32),
        vm((NX, NZ, 24) + tile, bf16),
        vm((NX, NZ, 12) + tile, jnp.int16),
    ]
    for shape, n in (
        ((2, NZ), NA), ((2, NZ), 2 * NA), ((2,), NA), ((2, 3), 2 * NA),
        ((2, NX), NB), ((2, 3, NX), 2 * NB), ((2,), NB), ((2,), 2 * NB),
    ):
        scratch += [vm(shape + (n,) + tile, bf16), vm(shape + (n // 2,) + tile, jnp.int16)]
    scratch += [
        vm((2, 64, 32, 128), bf16),
        vm((8, 128), jnp.int32),
        vm((2,) + tile, f32),
        vm((8,) + tile, f32),
        vm((128, 128), f32),
        vm((32, 1, 128), f32),
        vm((31, 1, 128), f32),
        dma((9,)),
    ]
    scratch += [dma((NX, NZ))] * 2
    for shape in ((2, NZ), (2, NZ), (2,), (2, 3), (2, NX), (2, 3, NX), (2,), (2,)):
        scratch += [dma(shape + (2,))] * 2
    scratch += [dma(())] * 8 + [pltpu.SemaphoreType.REGULAR] * 2
    return pl.pallas_call(
        main_kernel,
        out_shape=jax.ShapeDtypeStruct((1, 64), f32),
        in_specs=[
            pl.BlockSpec(memory_space=pl.ANY)
        ] * 6,
        out_specs=pl.BlockSpec(memory_space=pltpu.VMEM),
        scratch_shapes=scratch,
        compiler_params=pltpu.CompilerParams(
            collective_id=0, has_side_effects=True, vmem_limit_bytes=60 << 20
        ),
        name="rotor",
    )(directions.T, dest.T, bins.T, density, flow_rest, weights)


def solution(mesh):
    placed = (
        P("blk", "tm", None),
        P("blk", None, "tm", None),
        P("blk", None),
        P("blk", None, "tm", None),
        P(),
        P(None, "blk"),
    )
    return jax.shard_map(
        body, mesh=mesh, in_specs=placed, out_specs=P("blk", "tm"), check_vma=False
    )
```

```python
import jax
import jax.numpy as jnp
from jax import lax
from jax.experimental import pallas as pl
from jax.experimental.pallas import tpu as pltpu
from jax.sharding import PartitionSpec as P

NX, NZ, NY = 4, 8, 4
ROWS_DEV = 96
SLOTS = 4
NA = 8
NB = 12 - NA
TILES = [(0, i) for i in range(6)] + [(1, i) for i in (5, 4, 3, 2, 1, 0)]
A0, A1, A2 = 0, NA, 2 * NA
B0, B1, B2 = 2 * NA, 2 * NA + NB, 2 * NA + 2 * NB
MESH = pl.DeviceIdType.MESH
STEPS = 32512.0


def place(j, tile):
    if tile < NA:
        return j * NA + tile
    return 2 * NA + j * NB + tile - NA


def far_first(i, n):
    step = (i + 1) // 2
    return (n // 2 + step * (1 - 2 * (i % 2))) % n


def encode(x0, x1):
    parts, steps = [], []
    for x in (x0, x1):
        hi = x.astype(jnp.bfloat16)
        wide = hi.astype(jnp.float32)
        ratio = (x - wide) / jnp.where(wide == 0.0, 1.0, wide)
        parts.append(hi)
        steps.append((ratio * STEPS + 128.5).astype(jnp.int32))
    return parts[0], parts[1], ((steps[0] - 128) * 256 + steps[1]).astype(jnp.int16)


def decode(hi0, hi1, low):
    low = low.astype(jnp.int32)
    out = []
    for hi, step in ((hi0, low >> 8), (hi1, (low & 255) - 128)):
        out.append(hi.astype(jnp.float32) * (1.0 + step.astype(jnp.float32) * (1.0 / STEPS)))
    return out


def main_kernel(
    dir_hbm, dest_hbm, bins_hbm, dens_hbm, flow_hbm, wts_hbm, out_ref,
    dir_ref, dest_ref, bins_ref, dens_own, flow_own, dens_mate, flow_mate, list_vm, list_ref, lag_ref, C, S, R0, HC, LC, RA1, LA1, RA2, LA2, RA3, LA3, RA4, LA4,
    RB1, LB1, RB2, LB2, RB3, LB3, RB4, LB4, W, lag2, Z, G, M, HS, HR,
    ld_sem, s0, r0, sa1, ra1, sa2, ra2, sa3, ra3, sa4, ra4,
    sb1, rb1, sb2, rb2, sb3, rb3, sb4, rb4, sw, rw, sl, rl, sg, rg, sh, rh, met_y, met_mate,
):
    blk = lax.axis_index("blk")
    yy = lax.axis_index("tm")
    c = blk % 2
    chip = blk // 2
    z = chip % NZ
    x = chip // NZ

    def dev(dx, dz, core):
        return (((x + dx) % NX) * NZ + (z + dz) % NZ) * 2 + core

    near_x = (dev(1, 0, c), dev(NX - 1, 0, c))
    near_z = (dev(0, 1, c), dev(0, NZ - 1, c))
    mate = dev(0, 0, 1 - c)

    def remote(src, dst, ssem, rsem, to, ty=None):
        return pltpu.make_async_remote_copy(
            src_ref=src, dst_ref=dst, send_sem=ssem, recv_sem=rsem,
            device_id=(to, yy if ty is None else ty), device_id_type=MESH,
        )

    barrier = pltpu.get_barrier_semaphore()
    along_y = ((yy + 1) % NY, (yy + NY - 1) % NY)
    for to in near_x + near_z + (mate,):
        pl.semaphore_signal(barrier, inc=1, device_id=(to, yy), device_id_type=MESH)
    for to in along_y:
        pl.semaphore_signal(barrier, inc=1, device_id=(blk, to), device_id_type=MESH)

    small = [
        pltpu.make_async_copy(dest_hbm, dest_ref, ld_sem.at[4]),
        pltpu.make_async_copy(bins_hbm, bins_ref, ld_sem.at[5]),
        pltpu.make_async_copy(dir_hbm, dir_ref, ld_sem.at[6]),
    ]
    def half(core):
        return pl.ds(pl.multiple_of(core * 32, 32), 32)

    def row_loads(core, dens, flow, at):
        rows = pl.ds(0, ROWS_DEV)
        return [
            pltpu.make_async_copy(dens_hbm.at[:, half(core), :], dens.at[rows], ld_sem.at[at]),
            pltpu.make_async_copy(flow_hbm.at[:, :, half(core), :], flow.at[rows], ld_sem.at[at + 1]),
        ]

    loads_mate = row_loads(1 - c, dens_mate, flow_mate, 0)
    loads_own = row_loads(c, dens_own, flow_own, 7)
    own_wts = pltpu.make_async_copy(wts_hbm.at[0, :, half(c), :], W.at[c], ld_sem.at[2])
    for copy in small + loads_mate + loads_own + [own_wts]:
        copy.start()
    small[0].wait()
    small[1].wait()

    target = jnp.broadcast_to(dest_ref[...], (64, ROWS_DEV))
    hit = target == lax.broadcasted_iota(jnp.int32, (64, ROWS_DEV), 0)
    earlier = lax.broadcasted_iota(jnp.int32, (ROWS_DEV, ROWS_DEV), 0) < lax.broadcasted_iota(
        jnp.int32, (ROWS_DEV, ROWS_DEV), 1
    )

    def exact(flags):
        return jnp.where(flags, 1.0, 0.0).astype(jnp.bfloat16)

    before = jnp.dot(exact(hit), exact(earlier), preferred_element_type=jnp.float32)
    lane96 = lax.broadcasted_iota(jnp.int32, (ROWS_DEV, 128), 1)
    number = lax.broadcasted_iota(jnp.int32, (ROWS_DEV, 128), 0) - ROWS_DEV
    lists = jnp.full((64, 128), float(ROWS_DEV), jnp.float32)
    for s in range(SLOTS):
        column = jnp.where(lane96 == s, number, 0).astype(jnp.float32).astype(jnp.bfloat16)
        lists = lists + jnp.dot(
            exact(hit & (before == float(s))), column, preferred_element_type=jnp.float32
        )
    lists = jnp.clip(lists.astype(jnp.int32), 0, ROWS_DEV)
    lane64 = lax.broadcasted_iota(jnp.int32, (64, 128), 1)
    list_vm[...] = lists
    list_copy = pltpu.make_async_copy(list_vm, list_ref, ld_sem.at[3])
    list_copy.start()

    source = lax.broadcasted_iota(jnp.int32, (64, 128), 0)
    wanted = 2 * (lane64 % 32) + lane64 // 64
    spread = exact(source == wanted)
    lag_ref[...] = jnp.dot(
        jnp.broadcast_to(bins_ref[...], (8, 64)).astype(jnp.float32).astype(jnp.bfloat16),
        spread,
        preferred_element_type=jnp.float32,
    ).astype(jnp.int32)

    for dens, flow in ((dens_own, flow_own), (dens_mate, flow_mate)):
        dens[ROWS_DEV] = jnp.zeros((32, 128), jnp.bfloat16)
        flow[ROWS_DEV] = jnp.zeros((4, 32, 128), jnp.bfloat16)

    pl.semaphore_wait(barrier, 7)
    for to in along_y:
        pl.semaphore_signal(met_y, inc=1, device_id=(blk, to), device_id_type=MESH)

    wts_copy = remote(
        wts_hbm.at[0, :, pl.ds(pl.multiple_of((1 - c) * 32, 32), 32), :], W.at[c], sw, rw, mate
    )
    lag_copy = remote(lag_ref, lag2, sl, rl, mate)

    list_copy.wait()
    for copy in loads_mate:
        copy.wait()

    def core_copy(dx, dz):
        return remote(S.at[dx, dz], R0.at[dx, dz], s0.at[dx, dz], r0.at[dx, dz], mate)

    def unit(dx, dz, part):
        first = dev(dx, dz, 0)
        target = C if part == 0 else S
        dens, flow = (dens_own, flow_own) if part == 0 else (dens_mate, flow_mate)
        for j in range(2):
            rows = [list_ref[first + j, s] for s in range(SLOTS)]
            for chunk in range(2):
                span = pl.ds(chunk * 16, 16)
                acc = None
                for r in rows:
                    rho = dens[r, span, :].astype(jnp.float32)
                    u = flow[r, 0, span, :].astype(jnp.float32)
                    v = flow[r, 1, span, :].astype(jnp.float32)
                    w = flow[r, 2, span, :].astype(jnp.float32)
                    e = flow[r, 3, span, :].astype(jnp.float32)
                    ru, rv, rw_ = rho * u, rho * v, rho * w
                    terms = [ru * u, rv * v, rw_ * w, ru * v, ru * w, rv * w, e]
                    acc = terms if acc is None else [p + q for p, q in zip(acc, terms)]
                sums = [acc[0] + acc[6], acc[1] + acc[6], acc[2] + acc[6], acc[3], acc[4], acc[5]]
                for tile, (ch, comp) in enumerate(TILES):
                    if ch == chunk:
                        target[dx, dz, place(j, tile)] = sums[comp]
        if part == 1:
            core_copy(dx, dz).start()

    def combine(dx, dz, spans, send):
        for lo, hi, came in spans:

            def pair(p, carry):
                t = lo + 2 * p
                sums = [C[dx, dz, t], C[dx, dz, t + 1]]
                for hi_ref, low_ref, start in came:
                    k = t - start
                    more = decode(hi_ref[k], hi_ref[k + 1], low_ref[(lo - start) // 2 + p])
                    sums = [q + r for q, r in zip(sums, more)]
                if send:
                    h0, h1, low = encode(*sums)
                    HC[dx, dz, t] = h0
                    HC[dx, dz, t + 1] = h1
                    LC[dx, dz, lo // 2 + p] = low
                else:
                    C[dx, dz, t] = sums[0]
                    C[dx, dz, t + 1] = sums[1]
                return carry

            lax.fori_loop(0, (hi - lo) // 2, pair, 0, unroll=4)

    half_a = ((A0, A1), (A1, A2))
    half_b = ((B0, B1), (B1, B2))

    class Message:
        def __init__(self, dx, dz, span, hi_ref, low_ref, ssem, rsem, to):
            lo, n = span[0], span[1] - span[0]
            self.copies = [
                remote(HC.at[dx, dz, pl.ds(lo, n)], hi_ref, ssem(0), rsem(0), to),
                remote(LC.at[dx, dz, pl.ds(lo // 2, n // 2)], low_ref, ssem(1), rsem(1), to),
            ]
            self.came = (hi_ref, low_ref, lo)

        def start(self):
            for copy in self.copies:
                copy.start()

        def wait_send(self):
            for copy in self.copies:
                copy.wait_send()

        def wait_recv(self):
            for copy in self.copies:
                copy.wait_recv()
            return self.came

    def message(dx, dz, span, hi_ref, low_ref, ssem, rsem, to, *at):
        return Message(
            dx, dz, span, hi_ref.at[at], low_ref.at[at],
            lambda i: ssem.at[at + (i,)], lambda i: rsem.at[at + (i,)], to,
        )

    def m_a1(d, dz):
        return message(2, dz, half_a[d], RA1, LA1, sa1, ra1, near_x[d], d, dz)

    def m_a2(d, dz):
        return message(1 if d == 0 else 3, dz, (A0, A2), RA2, LA2, sa2, ra2, near_x[d], d, dz)

    def m_a3(d):
        return message(0, 4, half_a[d], RA3, LA3, sa3, ra3, near_z[d], d)

    def m_a4(d, k):
        dz = 3 - k if d == 0 else 5 + k
        return message(0, dz, (A0, A2), RA4, LA4, sa4, ra4, near_z[d], d, k)

    def m_b1(d, dx):
        return message(dx, 4, half_b[d], RB1, LB1, sb1, rb1, near_z[d], d, dx)

    def m_b2(d, k, dx):
        dz = 3 - k if d == 0 else 5 + k
        return message(dx, dz, (B0, B2), RB2, LB2, sb2, rb2, near_z[d], d, k, dx)

    def m_b3(d):
        return message(2, 0, half_b[d], RB3, LB3, sb3, rb3, near_x[d], d)

    def m_b4(d):
        return message(1 if d == 0 else 3, 0, (B0, B2), RB4, LB4, sb4, rb4, near_x[d], d)

    def halves(pair, d, extra, both=()):
        return [(lo, hi, list(both) + ([extra] if i == d else [])) for i, (lo, hi) in enumerate(pair)]

    def finish(gp):
        dz = far_first(gp, NZ)

        def step(k, carry):
            dx = far_first(k, NX)
            core_copy(dx, dz).wait_recv()
            C[dx, dz] = C[dx, dz] + R0[dx, dz]

            @pl.when(k == 0)
            def _():
                for d in range(2):
                    combine(2, dz, [half_a[d] + ((),)], True)
                    m_a1(d, dz).start()

            @pl.when(gp == 0)
            def _():
                for d in range(2):
                    combine(dx, 4, [half_b[d] + ((),)], True)
                    m_b1(d, dx).start()

            return carry

        lax.fori_loop(0, NX, step, 0)

    def ev_a2(dz):
        for d in range(2):
            came = m_a1(d, dz).wait_recv()
            combine(1 if d == 0 else 3, dz, halves(half_a, d, came), True)
            m_a2(d, dz).start()

    def ev_b2(k, dx):
        for d in range(2):
            dz = 3 - k if d == 0 else 5 + k
            if k == 0:
                spans = halves(half_b, d, m_b1(d, dx).wait_recv())
            else:
                spans = [(B0, B2, [m_b2(d, k - 1, dx).wait_recv()])]
            combine(dx, dz, spans, True)
            m_b2(d, k, dx).start()

    def ev_ra2(dz):
        both = [m_a2(0, dz).wait_recv(), m_a2(1, dz).wait_recv()]
        if dz == 4:
            combine(0, 4, [(A0, A2, both)], True)
            m_a3(0).start()
            m_a3(1).start()
        elif dz == 0:
            both += [m_a4(0, 2).wait_recv(), m_a4(1, 2).wait_recv()]
            combine(0, 0, [(A0, A2, both)], False)
        else:
            d, k = (0, 3 - dz) if dz < 4 else (1, dz - 5)
            if k == 0:
                spans = halves(half_a, d, m_a3(d).wait_recv(), both)
            else:
                spans = [(A0, A2, both + [m_a4(d, k - 1).wait_recv()])]
            combine(0, dz, spans, True)
            m_a4(d, k).start()

    def ev_rb2(dx):
        both = [m_b2(0, 2, dx).wait_recv(), m_b2(1, 2, dx).wait_recv()]
        if dx == 2:
            combine(2, 0, [(B0, B2, both)], True)
            m_b3(0).start()
            m_b3(1).start()
        elif dx == 0:
            both += [m_b4(0).wait_recv(), m_b4(1).wait_recv()]
            combine(0, 0, [(B0, B2, both)], False)
        else:
            d = 0 if dx == 1 else 1
            combine(dx, 0, halves(half_b, d, m_b3(d).wait_recv(), both), True)
            m_b4(d).start()

    def group(g, carry):
        dz = far_first(g, NZ)

        def across(k, inner):
            unit(far_first(k, NX), dz, 1)
            return inner

        def ahead(k, inner):
            unit(far_first(k, NX), far_first(g + 1, NZ), 1)
            return inner

        def own(k, inner):
            unit(far_first(k, NX), dz, 0)
            return inner

        @pl.when(g == 0)
        def _():
            lax.fori_loop(0, NX, across, 0)
            for copy in loads_own:
                copy.wait()

        @pl.when(g < NZ - 1)
        def _():
            lax.fori_loop(0, NX, ahead, 0)

        lax.fori_loop(0, NX, own, 0)

        finish(g)

        for step in range(2):

            @pl.when(g == 2 + 3 * step)
            def _(step=step):
                def send(k, inner):
                    ev_b2(step, far_first(k, NX))
                    return inner

                lax.fori_loop(0, NX, send, 0)

        @pl.when(g >= 3)
        def _():
            ev_a2(far_first(g - 3, NZ))

        return carry

    lax.fori_loop(0, NZ, group, 0)
    wts_copy.start()
    lag_copy.start()
    pl.semaphore_wait(met_y, 2)
    pl.semaphore_signal(met_mate, inc=1, device_id=(mate, yy), device_id_type=MESH)
    ev_b2(2, 2)
    ev_b2(2, 1)
    ev_ra2(4)
    ev_a2(1)
    ev_b2(2, 3)
    ev_ra2(3)
    ev_b2(2, 0)
    ev_ra2(5)
    ev_rb2(2)
    ev_a2(7)
    ev_ra2(2)
    ev_ra2(6)
    ev_a2(0)
    ev_rb2(1)
    ev_rb2(3)
    ev_ra2(1)
    ev_ra2(7)
    ev_rb2(0)
    ev_ra2(0)

    own_wts.wait()
    small[2].wait()
    wts_copy.wait()
    lag_copy.wait()
    lane16 = lax.broadcasted_iota(jnp.int32, (16, 128), 1)

    def project(o, carry):
        d0, d1, d2 = dir_ref[0, o], dir_ref[1, o], dir_ref[2, o]
        coef = [d0 * d0, d1 * d1, d2 * d2, 2.0 * d0 * d1, 2.0 * d0 * d2, 2.0 * d1 * d2]
        new = []
        for chunk in range(2):
            out = carry[chunk]
            for j in range(2):
                moment = None
                for tile, (ch, comp) in enumerate(TILES):
                    if ch == chunk:
                        term = coef[comp] * C[0, 0, place(j, tile)]
                        moment = term if moment is None else moment + term
                weight = W[j, o, pl.ds(chunk * 16, 16), :].astype(jnp.float32)
                value = jnp.sum(weight * moment, axis=1, keepdims=True)
                out = jnp.where(lane16 == (o % 2) * 64 + j * 32 + o // 2, value, out)
            new.append(out)
        return tuple(new)

    zero = jnp.zeros((16, 128), jnp.float32)
    cols = lax.fori_loop(0, 64, project, (zero, zero), unroll=16)

    low = lane16 < 64
    Z[0] = jnp.where(low, cols[0], pltpu.roll(cols[1], 64, 1))
    Z[1] = jnp.where(low, pltpu.roll(cols[0], 64, 1), cols[1])
    pl.semaphore_wait(met_mate, 1)
    mine = yy * 2 + c
    for dy in (2, 1, 3, 0):
        for dc in range(2):
            core = (c + dc) % 2
            if dy or dc:
                remote(Z.at[core], G.at[mine], sg, rg, chip * 2 + core, (yy + dy) % NY).start()
    G[mine] = Z[c]
    gathered = remote(G.at[pl.ds(0, 7)], G.at[pl.ds(0, 7)], sg, rg, mate)
    gathered.wait_recv()

    held = G[...]
    period = jnp.concatenate([held, pltpu.roll(held, 64, 2)], axis=1).reshape(256, 128)
    curved = pltpu.roll(period, 255, 0) - 2.0 * period + pltpu.roll(period, 1, 0)
    lane = lax.broadcasted_iota(jnp.int32, (8, 128), 1)
    own_half = jnp.where((lane // 32) % 2 == c, lag_ref[...], lag2[...])
    lags = jnp.where(lane // 64 == c, own_half, 0)
    lags = lags + pltpu.roll(lags, 64, 1)
    lags = ((lags + 256 - yy * 64) % 256)[0:1, :]
    shifted = curved
    for bit in range(8):
        chosen = jnp.broadcast_to((lags // (1 << bit)) % 2 == 1, (256, 128))
        shifted = jnp.where(chosen, pltpu.roll(shifted, 1 << bit, 0), shifted)
    slab = shifted[0:64, :]
    slab = slab + pltpu.roll(slab, 96, 1)
    M[...] = jnp.transpose(jnp.concatenate([slab, slab], axis=0))
    for i in range(32):
        HS[i] = M[pl.ds(i, 1), :]

    def send(i, carry):
        dx, dz = far_first(i // NZ, NX), far_first(i % NZ, NZ)
        to = dev(dx, dz, c)
        remote(HS.at[to // 2], HR.at[dx * NZ + dz - 1], sh, rh, to).start()
        return carry

    lax.fori_loop(0, NX * NZ - 1, send, 0)

    wait_all = [core_copy(i, j) for i in range(NX) for j in range(NZ)]
    wait_all += [m_a1(d, j) for d in range(2) for j in range(NZ)]
    wait_all += [m_a2(d, j) for d in range(2) for j in range(NZ)]
    wait_all += [m_a3(d) for d in range(2)]
    wait_all += [m_a4(d, k) for d in range(2) for k in range(3)]
    wait_all += [m_b1(d, i) for d in range(2) for i in range(NX)]
    wait_all += [m_b2(d, k, i) for d in range(2) for k in range(3) for i in range(NX)]
    wait_all += [m_b3(d) for d in range(2)]
    wait_all += [m_b4(d) for d in range(2)]
    gathered.wait_send()
    for copy in wait_all:
        copy.wait_send()

    own = HS[chip]
    scattered = remote(HS.at[pl.ds(0, 31)], HR.at[pl.ds(0, 31)], sh, rh, mate)
    scattered.wait_send()
    scattered.wait_recv()
    total = own + jnp.sum(HR[...], axis=0)
    out_ref[...] = total[:, 0:64]


def body(density, flow_rest, dest, weights, directions, bins):
    f32, bf16 = jnp.float32, jnp.bfloat16
    vm, dma = pltpu.VMEM, pltpu.SemaphoreType.DMA
    tile = (16, 128)
    scratch = [
        pltpu.SMEM((3, 64), f32),
        vm((1, ROWS_DEV), jnp.int32),
        vm((1, 64), jnp.int32),
        vm((ROWS_DEV + 1, 32, 128), bf16),
        vm((ROWS_DEV + 1, 4, 32, 128), bf16),
        vm((ROWS_DEV + 1, 32, 128), bf16),
        vm((ROWS_DEV + 1, 4, 32, 128), bf16),
        vm((64, 128), jnp.int32),
        pltpu.SMEM((64, 128), jnp.int32),
        vm((8, 128), jnp.int32),
        vm((NX, NZ, 24) + tile, f32),
        vm((NX, NZ, 24) + tile, f32),
        vm((NX, NZ, 24) + tile, f32),
        vm((NX, NZ, 24) + tile, bf16),
        vm((NX, NZ, 12) + tile, jnp.int16),
    ]
    for shape, n in (
        ((2, NZ), NA), ((2, NZ), 2 * NA), ((2,), NA), ((2, 3), 2 * NA),
        ((2, NX), NB), ((2, 3, NX), 2 * NB), ((2,), NB), ((2,), 2 * NB),
    ):
        scratch += [vm(shape + (n,) + tile, bf16), vm(shape + (n // 2,) + tile, jnp.int16)]
    scratch += [
        vm((2, 64, 32, 128), bf16),
        vm((8, 128), jnp.int32),
        vm((2,) + tile, f32),
        vm((8,) + tile, f32),
        vm((128, 128), f32),
        vm((32, 1, 128), f32),
        vm((31, 1, 128), f32),
        dma((9,)),
    ]
    scratch += [dma((NX, NZ))] * 2
    for shape in ((2, NZ), (2, NZ), (2,), (2, 3), (2, NX), (2, 3, NX), (2,), (2,)):
        scratch += [dma(shape + (2,))] * 2
    scratch += [dma(())] * 8 + [pltpu.SemaphoreType.REGULAR] * 2
    return pl.pallas_call(
        main_kernel,
        out_shape=jax.ShapeDtypeStruct((1, 64), f32),
        in_specs=[
            pl.BlockSpec(memory_space=pl.ANY)
        ] * 6,
        out_specs=pl.BlockSpec(memory_space=pltpu.VMEM),
        scratch_shapes=scratch,
        compiler_params=pltpu.CompilerParams(
            collective_id=0, has_side_effects=True, vmem_limit_bytes=60 << 20
        ),
        name="rotor",
    )(directions.T, dest.T, bins.T, density, flow_rest, weights)


def solution(mesh):
    placed = (
        P("blk", "tm", None),
        P("blk", None, "tm", None),
        P("blk", None),
        P("blk", None, "tm", None),
        P(),
        P(None, "blk"),
    )
    return jax.shard_map(
        body, mesh=mesh, in_specs=placed, out_specs=P("blk", "tm"), check_vma=False
    )
```
